32 devices in a mesh: day: 2 (over x), sta: 16 (over z, y, core).
Axes of the slice: x: 2, y: 2, z: 4, core: 2. Of those that a mesh axis runs over, the one named last changes fastest.
Arguments:
- spectra: bfloat16 [256, 4, 2, 8192], P(('day', 'sta')), parts along dimension 0, may hold values from -6 to 6
- window_mask: int32 [256, 4], P(('day', 'sta')), parts along dimension 0, may hold values from 0 to 1, as said below
- pair_slots: int32 [32, 2], P('sta'), may hold values from -1 to 15, as said below
Outputs:
- stacks: bfloat16 [64, 8, 8, 1024], P(('day', 'sta')), parts along dimension 0
The draws below stay inside these ranges and needn't reach their ends.
There are 2 independent parts, one for each index of `day`. The reference program is written for one: setup_inputs(seed, part) draws one part's arguments, and reference() takes and returns one part's arrays. A program takes and returns all parts, laid end to end along the dimension named above; an argument that names none is the same for every part. Nothing has to cross between parts.
Inputs may be any that keep to these rules, and one draw needn't show every extreme that they name: `pair_slots`: row o * 2 + c is slot c of owner block o: either (-1, -1), an empty slot, or two blocks a <= b, each within 2 blocks of o. An owner's live slots come before its empty ones; some owner fills all 2 slots and some owner has none. `window_mask`: in every draw some stations have no valid window at all.
All inputs are finite; a program needn't handle non-finite values.
Results may differ from the reference program's by a relative error of at most 0.0047.
Values may be sent and summed in bfloat16 or wider, within the bound.
No kernel may reach another device: no remote copies, remote signals or barrier semaphores. Data moves between devices by JAX's collectives and lax.ppermute only.
A program may use at most 128 MiB of HBM per device.

```python
import math
import jax
import jax.numpy as jnp
from jax import lax

STA_DEV = 8
WINDOWS = 4
FREQS = 8192
LAGS = 1024
CAP = 2
REACH = 2
NBLOCKS = 16
STATIONS = 128
TOTAL_PAIR_SLOTS = 32


def draw_window_mask(key, part):
    keys = jax.random.split(jax.random.fold_in(key, 11), 4)
    valid = (jax.random.randint(keys[0], (STATIONS, WINDOWS), 0, 4) < 3).astype(jnp.int32)
    dead_pick = jax.random.randint(keys[1], (NBLOCKS,), 0, STA_DEV)
    dead_block = jax.random.randint(keys[2], (NBLOCKS,), 0, 2) == 1
    forced_block = jax.random.randint(keys[3], (), 0, NBLOCKS)
    dead_block = dead_block | (jnp.arange(NBLOCKS, dtype=jnp.int32) == forced_block)
    station_in_block = jnp.arange(STA_DEV, dtype=jnp.int32)[None, :]
    silent = (station_in_block == dead_pick[:, None]) & dead_block[:, None]
    silent = silent.reshape(STATIONS)
    return jnp.where(silent[:, None], 0, valid).astype(jnp.int32)


def draw_pair_slots(key, part):
    keys = jax.random.split(jax.random.fold_in(key, 7), 5)
    owners = jnp.arange(NBLOCKS, dtype=jnp.int32)
    active_count = jax.random.randint(keys[0], (NBLOCKS,), 0, CAP + 1)
    busiest = jax.random.randint(keys[1], (), 0, NBLOCKS)
    spare_owner = jax.random.randint(keys[2], (), 0, NBLOCKS - 1)
    spare_owner = jnp.where(spare_owner == busiest, (spare_owner + 1) % (NBLOCKS - 1), spare_owner)
    active_count = jnp.where(owners == busiest, CAP, active_count)
    active_count = jnp.where(owners == spare_owner, 0, active_count)
    active_count = jnp.where(owners == NBLOCKS - 1, jnp.maximum(active_count, 1), active_count)
    first_step = jax.random.randint(keys[3], (NBLOCKS, CAP), -REACH, REACH + 1)
    second_step = jax.random.randint(keys[4], (NBLOCKS, CAP), -REACH, REACH + 1)
    slot_index = jnp.arange(CAP, dtype=jnp.int32)[None, :]
    forced = (owners[:, None] == NBLOCKS - 1) & (slot_index == 0)
    second_step = jnp.where(forced, jnp.maximum(second_step, 0), second_step)
    first_block = jnp.clip(owners[:, None] + first_step, 0, NBLOCKS - 1)
    second_block = jnp.clip(owners[:, None] + second_step, 0, NBLOCKS - 1)
    lower_station_block = jnp.minimum(first_block, second_block)
    upper_station_block = jnp.maximum(first_block, second_block)
    is_live = slot_index < active_count[:, None]
    lower_station_block = jnp.where(is_live, lower_station_block, -1)
    upper_station_block = jnp.where(is_live, upper_station_block, -1)
    return jnp.stack([lower_station_block, upper_station_block], axis=-1).reshape(TOTAL_PAIR_SLOTS, 2).astype(jnp.int32)


def shard_levels(stream_key, shape, pieces, low, high):
    level, own = 1.0, jax.random.fold_in(stream_key, 6)
    for axis_at, shards_of in pieces:
        steps = jnp.exp(jax.random.uniform(jax.random.fold_in(own, axis_at), (shards_of,), jnp.float32, low / len(pieces), high / len(pieces)))
        level = level * jnp.repeat(steps, shape[axis_at] // shards_of).reshape([-1 if axis == axis_at else 1 for axis in range(len(shape))])
    return level


def normal_values(stream_key, shape, scale, limit, cuts=(), kind=jnp.bfloat16):
    array = scale * jax.random.normal(stream_key, shape, jnp.float32)
    if cuts:
        array = array * shard_levels(stream_key, shape, cuts, -0.22, 0.18)
    return jnp.clip(array, -limit, limit).astype(kind)


def setup_inputs(seed: int = 0, part: int = 0) -> dict:
    key_of = jax.random.split(jax.random.key(seed), 4)
    part_splits = jax.random.split(jax.random.fold_in(key_of[3], part), 4)
    return {
        "spectra": normal_values(part_splits[0], (STATIONS, WINDOWS, 2, FREQS), 1.0, 6.0, ((0, 16),)),
        "window_mask": draw_window_mask(jax.random.fold_in(jax.random.fold_in(key_of[3], part), 71), part),
        "pair_slots": draw_pair_slots(jax.random.fold_in(key_of[3], 71), part),
    }


def lag_table(leading_frequency, freq_count, frequency_values, lag_count):
    freq_index = leading_frequency + jnp.arange(freq_count, dtype=jnp.int32)
    lag_index = jnp.arange(lag_count, dtype=jnp.int32) - lag_count // 2
    phase_index = jnp.mod(freq_index[:, None] * lag_index[None, :], 2 * frequency_values)
    phase_angle = phase_index.astype(jnp.float32) * (math.pi / frequency_values)
    return jnp.stack([jnp.cos(phase_angle), -jnp.sin(phase_angle)], axis=0).astype(jnp.bfloat16)

def cross_spectrum(first_real, first_imag, second_real, second_imag):
    real_part = jnp.einsum('pwf,qwf->pqf', first_real, second_real) + jnp.einsum('pwf,qwf->pqf', first_imag, second_imag)
    imag_part = jnp.einsum('pwf,qwf->pqf', first_imag, second_real) - jnp.einsum('pwf,qwf->pqf', first_real, second_imag)
    return jnp.stack([real_part, imag_part], axis=2)

def reference(spectra, window_mask, pair_slots):
    blocks = spectra.reshape(NBLOCKS, STA_DEV, WINDOWS, 2, FREQS)
    block_masks = window_mask.reshape(NBLOCKS, STA_DEV, WINDOWS).astype(jnp.float32)
    lag_rows = lag_table(0, FREQS, FREQS, LAGS).astype(jnp.float32)

    def one_slot(pair_row):
        first_block = jnp.clip(pair_row[0], 0, NBLOCKS - 1).astype(jnp.int32)
        second_block = jnp.clip(pair_row[1], 0, NBLOCKS - 1).astype(jnp.int32)
        is_live = (pair_row[0] >= 0).astype(jnp.float32)
        first_mask = block_masks[first_block]
        second_mask = block_masks[second_block]
        first_spec = blocks[first_block].astype(jnp.float32)
        second_spectrum_rows = blocks[second_block].astype(jnp.float32)
        cross_spec = cross_spectrum(first_spec[:, :, 0] * first_mask[:, :, None], first_spec[:, :, 1] * first_mask[:, :, None], second_spectrum_rows[:, :, 0] * second_mask[:, :, None], second_spectrum_rows[:, :, 1] * second_mask[:, :, None]) * is_live
        cross_spec = lax.optimization_barrier(cross_spec.astype(jnp.bfloat16)).astype(jnp.float32)
        running = jnp.einsum('pqcf,cfl->pql', cross_spec, lag_rows)
        pair_counts = jnp.dot(first_mask.astype(jnp.bfloat16), second_mask.astype(jnp.bfloat16).T, preferred_element_type=jnp.float32)
        weight_scale = 1.0 / (math.sqrt(FREQS) * jnp.maximum(pair_counts, 1.0))
        return (running * weight_scale[:, :, None]).astype(jnp.bfloat16)
    return lax.map(one_slot, pair_slots)
```

```python
import functools
import math

import jax
import jax.numpy as jnp
from jax import lax
from jax.experimental import pallas as pl
from jax.experimental.pallas import tpu as pltpu
from jax.sharding import PartitionSpec as P

LAGS = 1024
REACH = 2
CHUNKS = 4
SUB = 512
FINE = 64
LANES = 128


def permute(array, pairs):
    return lax.ppermute(array, "sta", pairs)


def angle_tables(index, lag_half, frequency_values):
    lag_index = jnp.arange(1, lag_half + 1, dtype=jnp.int32)
    phase_index = jnp.mod(index[:, None] * lag_index[None, :], 2 * frequency_values)
    phase_angle = phase_index.astype(jnp.float32) * (math.pi / frequency_values)
    return jnp.cos(phase_angle), jnp.sin(phase_angle)


def table_kernel(fine_cos, fine_sin, coarse_cos, coarse_sin, cos_ref, sin_ref):
    rows = cos_ref.shape[0]
    fc = fine_cos[...]
    fs = fine_sin[...]
    for group in range(rows // FINE):
        cc = coarse_cos[group : group + 1, :]
        cs = coarse_sin[group : group + 1, :]
        at = pl.ds(group * FINE, FINE)
        cos_ref[at, :] = (cc * fc - cs * fs).astype(jnp.bfloat16)
        sin_ref[at, :] = (cs * fc + cc * fs).astype(jnp.bfloat16)


def lag_tables(start, count, frequency_values, lag_half):
    fine = angle_tables(jnp.arange(FINE, dtype=jnp.int32), lag_half, frequency_values)
    coarse = angle_tables(
        start + FINE * jnp.arange(count // FINE, dtype=jnp.int32), lag_half, frequency_values
    )
    step = SUB
    table = jax.ShapeDtypeStruct((count, lag_half), jnp.bfloat16)
    return pl.pallas_call(
        table_kernel,
        grid=(count // step,),
        in_specs=[pl.BlockSpec((FINE, lag_half), lambda i: (0, 0))] * 2
        + [pl.BlockSpec((step // FINE, lag_half), lambda i: (i, 0))] * 2,
        out_specs=[pl.BlockSpec((step, lag_half), lambda i: (i, 0))] * 2,
        out_shape=[table, table],
        cost_estimate=pl.CostEstimate(
            flops=6 * count * lag_half, bytes_accessed=4 * count * lag_half, transcendentals=0
        ),
        name="lag_tables",
    )(*fine, *coarse)


def chunk_kernel(
    slots_ref, own_ref, par_ref, near_ref, far_ref, cos_ref, sin_ref, *rest, windows, stations, slot_count, first
):
    if first:
        acc_ref, stage, real_rows, imag_rows = rest
    else:
        before_ref, acc_ref, stage, real_rows, imag_rows = rest
    step = pl.program_id(0)
    lag_half = cos_ref.shape[1]
    pairs = stations * stations

    @pl.when(step == 0)
    def _():
        if first:
            acc_ref[...] = jnp.zeros_like(acc_ref)
        else:
            acc_ref[...] = before_ref[...]

    views = [own_ref, par_ref, near_ref.at[0], near_ref.at[1], far_ref.at[0], far_ref.at[1]]
    for at, view in enumerate(views):
        for window in range(windows):
            stage[at, window] = view[window].astype(jnp.float32)

    wide = 256

    def one_slot(slot, carry):
        first_at = slots_ref[slot, 0]
        second_at = slots_ref[slot, 1]
        base = pl.multiple_of(slot * pairs, pairs)

        @pl.when(slots_ref[slot, 2] > 0)
        def _():
            live_slot(first_at, second_at, base)

        @pl.when((slots_ref[slot, 2] == 0) & (step == 0))
        def _():
            empty = jnp.zeros((pairs, real_rows.shape[1]), jnp.bfloat16)
            real_rows[pl.ds(base, pairs), :] = empty
            imag_rows[pl.ds(base, pairs), :] = empty

        return carry

    def live_slot(first_at, second_at, base):
        for tile in range(own_ref.shape[-1] // wide):
            lanes = pl.ds(tile * wide, wide)
            second = [
                [
                    stage[second_at, window, pl.ds(part * stations, stations), lanes]
                    for part in range(2)
                ]
                for window in range(windows)
            ]
            for couple in range(0, stations, 2):
                real_out = []
                imag_out = []
                for station in (couple, couple + 1):
                    real = imag = None
                    for window in range(windows):
                        xr = stage[first_at, window, pl.ds(station, 1), lanes]
                        xi = stage[first_at, window, pl.ds(stations + station, 1), lanes]
                        yr, yi = second[window]
                        r = xr * yr + xi * yi
                        i = xi * yr - xr * yi
                        real = r if real is None else real + r
                        imag = i if imag is None else imag + i
                    real_out.append(real)
                    imag_out.append(imag)
                rows = pl.ds(base + couple * stations, 2 * stations)
                real = jnp.concatenate(real_out, axis=0)
                imag = jnp.concatenate(imag_out, axis=0)
                real_rows[rows, lanes] = real.astype(jnp.bfloat16)
                imag_rows[rows, lanes] = imag.astype(jnp.bfloat16)
                total = real[:, :LANES]
                for lane in range(LANES, wide, LANES):
                    total = total + real[:, lane : lane + LANES]
                acc_ref[rows, pl.ds(2 * lag_half, LANES)] += total

    lax.fori_loop(0, slot_count, one_slot, 0)
    acc_ref[:, :lag_half] += jnp.dot(
        real_rows[...], cos_ref[...], preferred_element_type=jnp.float32
    )
    acc_ref[:, lag_half : 2 * lag_half] += jnp.dot(
        imag_rows[...], sin_ref[...], preferred_element_type=jnp.float32
    )


def chunk_call(at, slots, own, par, near, far, cos_table, sin_table, before, windows, stations):
    slot_count = slots.shape[0]
    count = cos_table.shape[0] // CHUNKS
    lag_half = cos_table.shape[1]
    steps = count // SUB
    rows = slot_count * stations * stations
    acc = jax.ShapeDtypeStruct((rows, 2 * lag_half + LANES), jnp.float32)
    acc_spec = pl.BlockSpec(acc.shape, lambda i, s: (0, 0))
    single = (windows, 2 * stations, SUB)
    in_specs = [
        pl.BlockSpec(single, lambda i, s: (0, 0, i)),
        pl.BlockSpec(single, lambda i, s: (0, 0, i + at * steps)),
        pl.BlockSpec((2,) + single, lambda i, s: (0, 0, 0, i)),
        pl.BlockSpec((2,) + single, lambda i, s: (0, 0, 0, i)),
        pl.BlockSpec((SUB, lag_half), lambda i, s: (i + at * steps, 0)),
        pl.BlockSpec((SUB, lag_half), lambda i, s: (i + at * steps, 0)),
    ]
    operands = [own, par, near, far, cos_table, sin_table]
    aliases = {}
    if before is not None:
        in_specs.append(acc_spec)
        operands.append(before)
        aliases = {len(operands): 0}
    return pl.pallas_call(
        functools.partial(
            chunk_kernel, windows=windows, stations=stations, slot_count=slot_count, first=before is None
        ),
        grid_spec=pltpu.PrefetchScalarGridSpec(
            num_scalar_prefetch=1,
            grid=(steps,),
            in_specs=in_specs,
            out_specs=acc_spec,
            scratch_shapes=[
                pltpu.VMEM((6, windows, 2 * stations, SUB), jnp.float32),
                pltpu.VMEM((rows, SUB), jnp.bfloat16),
                pltpu.VMEM((rows, SUB), jnp.bfloat16),
            ],
        ),
        out_shape=acc,
        input_output_aliases=aliases,
        cost_estimate=pl.CostEstimate(
            flops=4 * rows * count * lag_half, bytes_accessed=4 * count * lag_half, transcendentals=0
        ),
        name="cross_chunk",
    )(slots, *operands)


def finish_kernel(
    slots_ref, mine_ref, other_ref, own_ref, par_ref, near_ref, far_ref, out_ref, marks, *, windows, stations, norm
):
    lag_half = out_ref.shape[1] // 2
    pairs = stations * stations
    views = [own_ref, par_ref, near_ref.at[0], near_ref.at[1], far_ref.at[0], far_ref.at[1]]
    for at, view in enumerate(views):
        for window in range(windows):
            marks[at, window] = view[window].astype(jnp.float32)[:stations]
    half = 256
    rows_at = lax.broadcasted_iota(jnp.int32, (half, half), 0)
    lanes_at = lax.broadcasted_iota(jnp.int32, (half, half), 1)
    flip = (rows_at + lanes_at == half - 1).astype(jnp.bfloat16)
    lane = lax.broadcasted_iota(jnp.int32, (stations, lag_half), 1)
    for slot in range(out_ref.shape[0] // pairs):
        first_at = slots_ref[slot, 0]
        second_at = slots_ref[slot, 1]
        left_rows = []
        for station in range(stations):
            count = None
            for window in range(windows):
                term = marks[first_at, window, pl.ds(station, 1), :] * marks[second_at, window]
                count = term if count is None else count + term
            weight = 1.0 / (norm * jnp.maximum(count, 1.0))
            weight = weight[:, :1]
            rows = pl.ds(slot * pairs + station * stations, stations)
            even = mine_ref[rows, :lag_half] + other_ref[rows, :lag_half]
            odd = (
                mine_ref[rows, lag_half : 2 * lag_half] + other_ref[rows, lag_half : 2 * lag_half]
            )
            still = jnp.sum(
                mine_ref[rows, 2 * lag_half :] + other_ref[rows, 2 * lag_half :], axis=1, keepdims=True
            )
            right = pltpu.roll(even - odd, 1, 1)
            right = jnp.where(lane == 0, still, right)
            out_ref[rows, lag_half:] = (right * weight).astype(jnp.bfloat16)
            left_rows.append((even + odd) * weight)
        left = jnp.concatenate(left_rows, axis=0).astype(jnp.bfloat16)
        rows = pl.ds(slot * pairs, pairs)
        for start in range(0, lag_half, half):
            out_ref[rows, lag_half - start - half : lag_half - start] = jnp.dot(
                left[:, start : start + half], flip, preferred_element_type=jnp.float32
            ).astype(jnp.bfloat16)


def finish_call(slots, mine, other, own, par, near, far, at, par_at, windows, stations, frequency_values):
    rows = mine.shape[0]
    lag_count = mine.shape[1] - LANES
    single = (windows, 2 * stations, LANES)
    whole = pl.BlockSpec(mine.shape, lambda i, s: (0, 0))
    return pl.pallas_call(
        functools.partial(
            finish_kernel, windows=windows, stations=stations, norm=math.sqrt(frequency_values)
        ),
        grid_spec=pltpu.PrefetchScalarGridSpec(
            num_scalar_prefetch=1,
            grid=(1,),
            in_specs=[
                whole,
                whole,
                pl.BlockSpec(single, lambda i, s: (0, 0, at)),
                pl.BlockSpec(single, lambda i, s: (0, 0, par_at)),
                pl.BlockSpec((2,) + single, lambda i, s: (0, 0, 0, at)),
                pl.BlockSpec((2,) + single, lambda i, s: (0, 0, 0, at)),
            ],
            out_specs=pl.BlockSpec((rows, lag_count), lambda i, s: (0, 0)),
            scratch_shapes=[pltpu.VMEM((6, windows, stations, LANES), jnp.float32)],
        ),
        out_shape=jax.ShapeDtypeStruct((rows, lag_count), jnp.bfloat16),
        cost_estimate=pl.CostEstimate(
            flops=4 * rows * lag_count, bytes_accessed=10 * rows * lag_count, transcendentals=0
        ),
        name="finish",
    )(slots, mine, other, own, par, near, far)


def shards(spectra, window_mask, pair_slots):
    stations, windows, _, frequency_values = spectra.shape
    slot_count = pair_slots.shape[0]
    half = frequency_values // 2
    count = half // CHUNKS
    peers = lax.axis_size("sta")
    me = lax.axis_index("sta")
    core = me % 2
    chip = me // 2
    core_pairs = [(i, i ^ 1) for i in range(peers)]
    near_pairs = [(i, i ^ 2) for i in range(peers)]
    far_pairs = [
        (i, i + 4 - 8 * ((i // 2) % 2))
        for i in range(peers)
        if 0 <= i + 4 - 8 * ((i // 2) % 2) < peers
    ]
    valid = window_mask.astype(jnp.bfloat16).T[:, None, :, None]
    mark = jnp.broadcast_to(valid, (windows, 2, stations, LANES)).reshape(
        windows, 2 * stations, LANES
    )

    def rows_of(start, size):
        piece = lax.dynamic_slice_in_dim(spectra, start, size, 3)
        return (piece.transpose(1, 2, 0, 3) * valid).reshape(windows, 2 * stations, size)

    sent = jnp.concatenate([rows_of((1 - core) * half, half), mark], axis=2)
    par = permute(sent, core_pairs)
    other_slots = permute(pair_slots, core_pairs)
    own = [rows_of(core * half + at * count, count) for at in range(CHUNKS)]
    own[0] = jnp.concatenate([own[0], mark], axis=2)
    near = []
    for at in range(CHUNKS):
        piece = par[:, :, at * count : (at + 1) * count]
        if at == 0:
            piece = jnp.concatenate([piece, par[:, :, half:]], axis=2)
        near.append(permute(jnp.stack([own[at], piece]), near_pairs))
    far = [permute(piece, far_pairs) for piece in near]

    cos_table, sin_table = lag_tables(core * half, half, frequency_values, LAGS // 2)
    slots = jnp.concatenate([pair_slots, other_slots], axis=0)
    slot_chip = slots // 2
    group = jnp.where(slot_chip == chip, 0, jnp.where(slot_chip == (chip ^ 1), 1, 2))
    other_core = (slots % 2 != core).astype(jnp.int32)
    index = group * 2 + other_core
    live = (slots[:, :1] >= 0).astype(jnp.int32)
    table = jnp.concatenate([index, live], axis=1)
    acc = None
    for at in range(CHUNKS):
        acc = chunk_call(
            at, table, own[at], par, near[at], far[at], cos_table, sin_table, acc, windows, stations
        )
    rows = slot_count * stations * stations
    mine = acc[:rows]
    other = permute(acc[rows:], core_pairs)
    out = finish_call(
        table, mine, other, own[0], par, near[0], far[0], count // LANES, half // LANES, windows, stations, frequency_values
    )
    return out.reshape(slot_count, stations, stations, LAGS)


def solution(mesh):
    placed = (P(("day", "sta"), None, None, None), P(("day", "sta"), None), P("sta", None))
    return jax.shard_map(
        shards,
        mesh=mesh,
        in_specs=placed,
        out_specs=P(("day", "sta"), None, None, None),
        check_vma=False,
    )
```

```python
import functools
import math

import jax
import jax.numpy as jnp
from jax import lax
from jax.experimental import pallas as pl
from jax.experimental.pallas import tpu as pltpu
from jax.sharding import PartitionSpec as P


LAGS = 1024
CUTS = (0, 8, 12, 16)
SUB = 512
FINE = 64
LANES = 128
GRANT = 24 << 20


def permute(array, pairs):
    return lax.ppermute(array, "sta", pairs)


def angle_tables(index, lag_half, frequency_values):
    lag_index = jnp.arange(1, lag_half + 1, dtype=jnp.int32)
    phase_index = jnp.mod(index[:, None] * lag_index[None, :], 2 * frequency_values)
    phase_angle = phase_index.astype(jnp.float32) * (math.pi / frequency_values)
    return jnp.cos(phase_angle), jnp.sin(phase_angle)


def chunk_kernel(*refs, views_at, slot_count, windows, stations, first, last, low):
    refs = list(refs)
    slots_ref = refs.pop(0)
    sources = [refs.pop(0) for _ in range(1 + max(which for which, _, _ in views_at))]
    fine_cos, fine_sin, coarse_cos, coarse_sin = (refs.pop(0) for _ in range(4))
    before_ref = None if first else refs.pop(0)
    outs = [refs.pop(0) for _ in range(2 if last else 1)]
    stage, real_rows, imag_rows, cos_rows, sin_rows, still = refs
    count = stage.shape[-1]
    lag_half = cos_rows.shape[1]
    pairs = stations * stations
    rows = slot_count * pairs

    for at, (which, part, lane) in enumerate(views_at):
        view = sources[which] if part is None else sources[which].at[part]
        for window in range(windows):
            stage[at, window] = view[window, :, lane : lane + count].astype(jnp.float32)

    fc = fine_cos[...]
    fs = fine_sin[...]
    for group in range(count // FINE):
        coarse = slice(low // FINE + group, low // FINE + group + 1)
        cc = coarse_cos[coarse, :]
        cs = coarse_sin[coarse, :]
        at = pl.ds(group * FINE, FINE)
        cos_rows[at, :] = (cc * fc - cs * fs).astype(jnp.bfloat16)
        sin_rows[at, :] = (cs * fc + cc * fs).astype(jnp.bfloat16)

    def one_slot(slot, carry):
        base = pl.multiple_of(slot * pairs, pairs)
        still[pl.ds(base, pairs), :] = jnp.zeros((pairs, LANES), jnp.float32)

        @pl.when(slots_ref[slot, 2] > 0)
        def _():
            first_at = slots_ref[slot, 0]
            second_at = slots_ref[slot, 1]

            def one_sub(sub, carry):
                live_slot(first_at, second_at, base, sub * SUB)
                return carry

            lax.fori_loop(0, count // SUB, one_sub, 0)

        @pl.when(slots_ref[slot, 2] == 0)
        def _():
            empty = jnp.zeros((pairs, count), jnp.bfloat16)
            real_rows[pl.ds(base, pairs), :] = empty
            imag_rows[pl.ds(base, pairs), :] = empty

        return carry

    wide = 256

    def live_slot(first_at, second_at, base, start):
        for tile in range(SUB // wide):
            lanes = pl.ds(pl.multiple_of(start + tile * wide, wide), wide)
            second = [
                [
                    stage[second_at, window, pl.ds(part * stations, stations), lanes]
                    for part in range(2)
                ]
                for window in range(windows)
            ]
            for couple in range(0, stations, 2):
                real_out = []
                imag_out = []
                for station in (couple, couple + 1):
                    real = imag = None
                    for window in range(windows):
                        xr = stage[first_at, window, pl.ds(station, 1), lanes]
                        xi = stage[first_at, window, pl.ds(stations + station, 1), lanes]
                        yr, yi = second[window]
                        r = xr * yr + xi * yi
                        i = xi * yr - xr * yi
                        real = r if real is None else real + r
                        imag = i if imag is None else imag + i
                    real_out.append(real)
                    imag_out.append(imag)
                at = pl.ds(base + couple * stations, 2 * stations)
                real = jnp.concatenate(real_out, axis=0)
                imag = jnp.concatenate(imag_out, axis=0)
                real_rows[at, lanes] = real.astype(jnp.bfloat16)
                imag_rows[at, lanes] = imag.astype(jnp.bfloat16)
                total = real[:, :LANES]
                for lane in range(LANES, wide, LANES):
                    total = total + real[:, lane : lane + LANES]
                still[at, :] += total

    lax.fori_loop(0, slot_count, one_slot, 0)
    share = rows // len(outs)
    even = jnp.dot(real_rows[...], cos_rows[...], preferred_element_type=jnp.float32)
    odd = jnp.dot(imag_rows[...], sin_rows[...], preferred_element_type=jnp.float32)
    for lane, value in ((0, even), (lag_half, odd), (2 * lag_half, still[...])):
        lanes = slice(lane, lane + value.shape[1])
        if not first:
            value = value + before_ref[:, lanes]
        for at, out in enumerate(outs):
            out[:, lanes] = value[at * share : (at + 1) * share]


def chunk_call(slots, sources, views_at, tables, before, last, low, count, lag_half, windows, stations):
    slot_count = slots.shape[0]
    rows = slot_count * stations * stations
    outs = 2 if last else 1
    acc = jax.ShapeDtypeStruct((rows // outs, 2 * lag_half + LANES), jnp.float32)
    operands = list(sources) + list(tables)
    if before is not None:
        operands.append(before)
    vmem = pl.BlockSpec(memory_space=pltpu.VMEM)
    return pl.pallas_call(
        functools.partial(
            chunk_kernel,
            views_at=views_at,
            slot_count=slot_count,
            windows=windows,
            stations=stations,
            first=before is None,
            last=last,
            low=low,
        ),
        in_specs=[pl.BlockSpec(memory_space=pltpu.SMEM)] + [vmem] * len(operands),
        out_specs=[vmem] * outs,
        scratch_shapes=[
            pltpu.VMEM((6, windows, 2 * stations, count), jnp.float32),
            pltpu.VMEM((rows, count), jnp.bfloat16),
            pltpu.VMEM((rows, count), jnp.bfloat16),
            pltpu.VMEM((count, lag_half), jnp.bfloat16),
            pltpu.VMEM((count, lag_half), jnp.bfloat16),
            pltpu.VMEM((rows, LANES), jnp.float32),
        ],
        out_shape=[acc] * outs,
        input_output_aliases={} if before is None or last else {len(operands): 0},
        cost_estimate=pl.CostEstimate(
            flops=4 * rows * count * lag_half, bytes_accessed=4 * count * lag_half, transcendentals=0
        ),
        compiler_params=pltpu.CompilerParams(vmem_limit_bytes=GRANT),
    )(slots, *operands)


def finish_kernel(
    slots_ref, mine_ref, other_ref, own_ref, par_ref, near_own, near_par, far_own, far_par, out_ref, marks, *, windows, stations, norm
):
    lag_half = out_ref.shape[1] // 2
    pairs = stations * stations
    for at, view in enumerate([own_ref, par_ref, near_own, near_par, far_own, far_par]):
        for window in range(windows):
            marks[at, window] = view[window, :, :LANES].astype(jnp.float32)[:stations]
    half = 256
    rows_at = lax.broadcasted_iota(jnp.int32, (half, half), 0)
    lanes_at = lax.broadcasted_iota(jnp.int32, (half, half), 1)
    flip = (rows_at + lanes_at == half - 1).astype(jnp.bfloat16)
    lane = lax.broadcasted_iota(jnp.int32, (stations, lag_half), 1)
    for slot in range(out_ref.shape[0] // pairs):
        first_at = slots_ref[slot, 0]
        second_at = slots_ref[slot, 1]
        left_rows = []
        for station in range(stations):
            count = None
            for window in range(windows):
                term = marks[first_at, window, pl.ds(station, 1), :] * marks[second_at, window]
                count = term if count is None else count + term
            weight = 1.0 / (norm * jnp.maximum(count, 1.0))
            weight = weight[:, :1]
            rows = pl.ds(slot * pairs + station * stations, stations)
            even = mine_ref[rows, :lag_half] + other_ref[rows, :lag_half]
            odd = (
                mine_ref[rows, lag_half : 2 * lag_half] + other_ref[rows, lag_half : 2 * lag_half]
            )
            still = jnp.sum(
                mine_ref[rows, 2 * lag_half :] + other_ref[rows, 2 * lag_half :], axis=1, keepdims=True
            )
            right = pltpu.roll(even - odd, 1, 1)
            right = jnp.where(lane == 0, still, right)
            out_ref[rows, lag_half:] = (right * weight).astype(jnp.bfloat16)
            left_rows.append((even + odd) * weight)
        left = jnp.concatenate(left_rows, axis=0).astype(jnp.bfloat16)
        rows = pl.ds(slot * pairs, pairs)
        for start in range(0, lag_half, half):
            out_ref[rows, lag_half - start - half : lag_half - start] = jnp.dot(
                left[:, start : start + half], flip, preferred_element_type=jnp.float32
            ).astype(jnp.bfloat16)


def finish_call(slots, mine, other, marked, windows, stations, frequency_values):
    rows = mine.shape[0]
    lag_count = mine.shape[1] - LANES
    vmem = pl.BlockSpec(memory_space=pltpu.VMEM)
    return pl.pallas_call(
        functools.partial(
            finish_kernel, windows=windows, stations=stations, norm=math.sqrt(frequency_values)
        ),
        in_specs=[pl.BlockSpec(memory_space=pltpu.SMEM)] + [vmem] * 8,
        out_specs=vmem,
        scratch_shapes=[pltpu.VMEM((6, windows, stations, LANES), jnp.float32)],
        out_shape=jax.ShapeDtypeStruct((rows, lag_count), jnp.bfloat16),
        cost_estimate=pl.CostEstimate(
            flops=4 * rows * lag_count, bytes_accessed=10 * rows * lag_count, transcendentals=0
        ),
        compiler_params=pltpu.CompilerParams(vmem_limit_bytes=GRANT // 2),
        name="finish",
    )(slots, mine, other, *marked)


def owner_stacks(spectra, window_mask, pair_slots):
    stations, windows, _, frequency_values = spectra.shape
    slot_count = pair_slots.shape[0]
    half = frequency_values // 2
    lag_half = LAGS // 2
    peers = lax.axis_size("sta")
    me = lax.axis_index("sta")
    core = me & 1
    chip = me >> 1
    core_pairs = [(i, i ^ 1) for i in range(peers)]
    near_pairs = [(i, i ^ 2) for i in range(peers)]
    far_pairs = [
        (i, i + 4 - 8 * ((i // 2) % 2))
        for i in range(peers)
        if 0 <= i + 4 - 8 * ((i // 2) % 2) < peers
    ]
    valid = window_mask.astype(jnp.bfloat16).T[:, None, :, None]
    mark = jnp.broadcast_to(valid, (windows, 2, stations, LANES)).reshape(
        windows, 2 * stations, LANES
    )

    def rows_of(start, size):
        piece = lax.dynamic_slice_in_dim(spectra, start, size, 3)
        return (piece.transpose(1, 2, 0, 3) * valid).reshape(windows, 2 * stations, size)

    splits = [half * cut // 16 for cut in CUTS]
    lead = splits[1]
    own_lead = jnp.concatenate([mark, rows_of(core * half, lead)], axis=2)
    sent = jnp.concatenate([mark, rows_of((1 - core) * half, half)], axis=2)
    par = permute(sent, core_pairs)
    other_slots = permute(pair_slots, core_pairs)
    near = [permute(own_lead, near_pairs), permute(par[:, :, : LANES + lead], near_pairs)]
    own = []
    for at in range(1, len(splits) - 1):
        low, high = splits[at], splits[at + 1]
        own.append(rows_of(core * half + low, high - low))
        piece = jnp.stack([own[-1], par[:, :, LANES + low : LANES + high]])
        if high == half:
            piece, base = lax.optimization_barrier((piece, core * half))
        near.append(permute(piece, near_pairs))
    far = [permute(piece, far_pairs) for piece in near]

    fine = angle_tables(jnp.arange(FINE, dtype=jnp.int32), lag_half, frequency_values)
    coarse = angle_tables(
        base + FINE * jnp.arange(half // FINE, dtype=jnp.int32), lag_half, frequency_values
    )
    slots = jnp.concatenate([pair_slots, other_slots], axis=0)
    slot_chip = slots >> 1
    group = jnp.where(slot_chip == chip, 0, jnp.where(slot_chip == (chip ^ 1), 1, 2))
    other_core = ((slots & 1) != core).astype(jnp.int32)
    live = (slots[:, :1] >= 0).astype(jnp.int32)
    table = jnp.concatenate([group * 2 + other_core, live], axis=1)
    acc = None
    for at in range(len(splits) - 1):
        low, high = splits[at], splits[at + 1]
        last = at == len(splits) - 2
        if at == 0:
            sources = [own_lead, par, near[0], near[1], far[0], far[1]]
            views_at = [(which, None, LANES) for which in range(6)]
        else:
            sources = [own[at - 1], par, near[at + 1], far[at + 1]]
            views_at = [(0, None, 0), (1, None, LANES + low), (2, 0, 0), (2, 1, 0), (3, 0, 0), (3, 1, 0)]
        tables = list(fine) + list(coarse)
        acc = chunk_call(
            table, sources, views_at, tables, acc, last, low, high - low, lag_half, windows, stations
        )
        if not last:
            acc = acc[0]
    mine, other = acc
    other = permute(other, core_pairs)
    marked = [own_lead, par, near[0], near[1], far[0], far[1]]
    out = finish_call(table, mine, other, marked, windows, stations, frequency_values)
    return out.reshape(slot_count, stations, stations, LAGS)


def solution(mesh):
    placed = (P(("day", "sta"), None, None, None), P(("day", "sta"), None), P("sta", None))
    return jax.shard_map(
        owner_stacks,
        mesh=mesh,
        in_specs=placed,
        out_specs=P(("day", "sta"), None, None, None),
        check_vma=False,
    )
```

```python
import functools
import math

import jax
import jax.numpy as jnp
from jax import lax
from jax.experimental import pallas as pl
from jax.experimental.pallas import tpu as pltpu
from jax.sharding import PartitionSpec as P


LAGS = 1024
CUTS = (0, 8, 12, 16)
SUB = 512
FINE = 64
LANES = 128
GRANT = 24 << 20


def permute(array, pairs):
    return lax.ppermute(array, "sta", pairs)


def angle_tables(index, lag_half, frequency_values):
    lag_index = jnp.arange(1, lag_half + 1, dtype=jnp.int32)
    phase_index = jnp.mod(index[:, None] * lag_index[None, :], 2 * frequency_values)
    phase_angle = phase_index.astype(jnp.float32) * (math.pi / frequency_values)
    return jnp.cos(phase_angle), jnp.sin(phase_angle)


def table_kernel(fine_cos, fine_sin, coarse_cos, coarse_sin, cos_ref, sin_ref):
    fc = fine_cos[...]
    fs = fine_sin[...]

    def one_group(group, carry):
        cc = coarse_cos[pl.ds(group, 1), :]
        cs = coarse_sin[pl.ds(group, 1), :]
        at = pl.ds(pl.multiple_of(group * FINE, FINE), FINE)
        cos_ref[at, :] = (cc * fc - cs * fs).astype(jnp.bfloat16)
        sin_ref[at, :] = (cs * fc + cc * fs).astype(jnp.bfloat16)
        return carry

    lax.fori_loop(0, cos_ref.shape[0] // FINE, one_group, 0)


def lag_tables(fine, coarse):
    count = coarse[0].shape[0] * FINE
    lag_half = fine[0].shape[1]
    vmem = pl.BlockSpec(memory_space=pltpu.VMEM)
    table = jax.ShapeDtypeStruct((count, lag_half), jnp.bfloat16)
    return pl.pallas_call(
        table_kernel,
        in_specs=[vmem] * 4,
        out_specs=[vmem] * 2,
        out_shape=[table, table],
        compiler_params=pltpu.CompilerParams(vmem_limit_bytes=GRANT),
        cost_estimate=pl.CostEstimate(
            flops=6 * count * lag_half, bytes_accessed=4 * count * lag_half, transcendentals=0
        ),
        name="tables",
    )(*fine, *coarse)


def pair_weights(slots_ref, sources, marks, weight_ref, slot_count, windows, stations, norm):
    pairs = stations * stations
    for at, view in enumerate(sources):
        for window in range(windows):
            marks[at, window] = view[window, :, :LANES].astype(jnp.float32)[:stations]
    for slot in range(slot_count):
        first_at = slots_ref[slot, 0]
        second_at = slots_ref[slot, 1]
        live = slots_ref[slot, 2].astype(jnp.float32)
        for station in range(stations):
            count = None
            for window in range(windows):
                term = marks[first_at, window, pl.ds(station, 1), :] * marks[second_at, window]
                count = term if count is None else count + term
            rows = pl.ds(slot * pairs + station * stations, stations)
            weight_ref[rows, :] = live / (norm * jnp.maximum(count, 1.0))


def flip_matrix(size):
    rows_at = lax.broadcasted_iota(jnp.int32, (size, size), 0)
    lanes_at = lax.broadcasted_iota(jnp.int32, (size, size), 1)
    return (rows_at + lanes_at == size - 1).astype(jnp.bfloat16)


def lay_out(acc_ref, weight_ref, out_ref, start):
    rows = out_ref.shape[0]
    lag_half = out_ref.shape[1] // 2
    size = 256
    flip = flip_matrix(size)
    at = pl.ds(start, rows)
    even = acc_ref[at, :lag_half]
    odd = acc_ref[at, lag_half : 2 * lag_half]
    weight = weight_ref[at, :][:, :1]
    still = jnp.sum(acc_ref[at, 2 * lag_half :], axis=1, keepdims=True)
    lane = lax.broadcasted_iota(jnp.int32, (rows, lag_half), 1)
    right = jnp.where(lane == 0, still, pltpu.roll(even - odd, 1, 1))
    out_ref[:, lag_half:] = (right * weight).astype(out_ref.dtype)
    left = (even + odd) * weight
    parts = [left.astype(jnp.bfloat16)]
    if out_ref.dtype == jnp.float32:
        parts.append((left - parts[0].astype(jnp.float32)).astype(jnp.bfloat16))
    for lane in range(0, lag_half, size):
        flipped = sum(
            jnp.dot(part[:, lane : lane + size], flip, preferred_element_type=jnp.float32)
            for part in parts
        )
        out_ref[:, lag_half - lane - size : lag_half - lane] = flipped.astype(out_ref.dtype)


def chunk_kernel(*refs, views_at, slot_count, windows, stations, first, last, low, norm):
    refs = list(refs)
    slots_ref = refs.pop(0)
    sources = [refs.pop(0) for _ in range(1 + max(which for which, _, _ in views_at))]
    cos_ref, sin_ref = (refs.pop(0) for _ in range(2))
    if not first:
        before_ref = refs.pop(0)
    if last:
        weight_ref, mine_ref, theirs_ref = (refs.pop(0) for _ in range(3))
        acc_ref = refs.pop()
    else:
        acc_ref = refs.pop(0)
    if first:
        weight_ref = refs.pop(0)
        marks = refs.pop()
    stage = refs.pop(0)
    buffers = [(refs[0], refs[1]), (refs[2], refs[3])]
    count = stage.shape[-1]
    lag_half = cos_ref.shape[1]
    pairs = stations * stations
    width = buffers[0][0].shape[1]
    wide = 256

    if first:
        pair_weights(slots_ref, sources, marks, weight_ref, slot_count, windows, stations, norm)
        acc_ref[:, 2 * lag_half :] = jnp.zeros((slot_count * pairs, LANES), jnp.float32)
    else:
        acc_ref[:, 2 * lag_half :] = before_ref[:, 2 * lag_half :]

    for at, (which, part, lane) in enumerate(views_at):
        view = sources[which] if part is None else sources[which].at[part]
        for window in range(windows):
            stage[at, window] = view[window, :, lane : lane + count].astype(jnp.float32)

    index = [(slots_ref[slot, 0], slots_ref[slot, 1]) for slot in range(slot_count)]

    def cross(start, real_rows, imag_rows):
        for slot in range(slot_count):
            first_at, second_at = index[slot]
            for tile in range(width // wide):
                lanes = pl.ds(start + tile * wide, wide)
                held = pl.ds(tile * wide, wide)
                second = [
                    [
                        stage[second_at, window, pl.ds(part * stations, stations), lanes]
                        for part in range(2)
                    ]
                    for window in range(windows)
                ]
                for couple in range(0, stations, 2):
                    real_out = []
                    imag_out = []
                    for station in (couple, couple + 1):
                        real = imag = None
                        for window in range(windows):
                            xr = stage[first_at, window, pl.ds(station, 1), lanes]
                            xi = stage[first_at, window, pl.ds(stations + station, 1), lanes]
                            yr, yi = second[window]
                            r = xr * yr + xi * yi
                            i = xi * yr - xr * yi
                            real = r if real is None else real + r
                            imag = i if imag is None else imag + i
                        real_out.append(real)
                        imag_out.append(imag)
                    at = pl.ds(slot * pairs + couple * stations, 2 * stations)
                    real = jnp.concatenate(real_out, axis=0)
                    imag = jnp.concatenate(imag_out, axis=0)
                    real_rows[at, held] = real.astype(jnp.bfloat16)
                    imag_rows[at, held] = imag.astype(jnp.bfloat16)
                    total = real[:, :LANES]
                    for lane in range(LANES, wide, LANES):
                        total = total + real[:, lane : lane + LANES]
                    acc_ref[at, pl.ds(2 * lag_half, LANES)] += total

    def gather_lags(start, real_rows, imag_rows):
        at = pl.ds(low + start, width)
        for lane, rows, table in ((0, real_rows, cos_ref), (lag_half, imag_rows, sin_ref)):
            lanes = slice(lane, lane + lag_half)
            value = jnp.dot(rows[...], table[at, :], preferred_element_type=jnp.float32)
            if start > 0:
                value = value + acc_ref[:, lanes]
            elif not first:
                value = value + before_ref[:, lanes]
            acc_ref[:, lanes] = value

    steps = count // width
    for step in range(steps):
        cross(step * width, *buffers[step % 2])
        if step > 0:
            gather_lags((step - 1) * width, *buffers[(step - 1) % 2])
    gather_lags((steps - 1) * width, *buffers[(steps - 1) % 2])
    if last:
        half = slot_count * pairs // 2
        lay_out(acc_ref, weight_ref, theirs_ref, half)
        mine_ref[...] = acc_ref[:half, :]


def chunk_call(slots, sources, views_at, tables, before, weights, last, low, count, width, windows, stations, norm):
    slot_count = slots.shape[0]
    lag_half = tables[0].shape[1]
    rows = slot_count * stations * stations
    first = before is None
    acc = jax.ShapeDtypeStruct((rows, 2 * lag_half + LANES), jnp.float32)
    operands = list(sources) + list(tables)
    if not first:
        operands.append(before)
    if last:
        operands.append(weights)
    vmem = pl.BlockSpec(memory_space=pltpu.VMEM)
    scratch = [pltpu.VMEM((6, windows, 2 * stations, count), jnp.float32)]
    scratch += [pltpu.VMEM((rows, width), jnp.bfloat16)] * 4
    outs = [acc]
    if first:
        outs.append(jax.ShapeDtypeStruct((rows, LANES), jnp.float32))
        scratch.append(pltpu.VMEM((6, windows, stations, LANES), jnp.float32))
    if last:
        outs = [
            jax.ShapeDtypeStruct((rows // 2, 2 * lag_half + LANES), jnp.float32),
            jax.ShapeDtypeStruct((rows // 2, 2 * lag_half), jnp.bfloat16),
        ]
        scratch.append(pltpu.VMEM(acc.shape, jnp.float32))
    return pl.pallas_call(
        functools.partial(
            chunk_kernel,
            views_at=views_at,
            slot_count=slot_count,
            windows=windows,
            stations=stations,
            first=first,
            last=last,
            low=low,
            norm=norm,
        ),
        in_specs=[pl.BlockSpec(memory_space=pltpu.SMEM)] + [vmem] * len(operands),
        out_specs=[vmem] * len(outs),
        scratch_shapes=scratch,
        out_shape=outs,
        input_output_aliases={} if first or last else {len(operands): 0},
        cost_estimate=pl.CostEstimate(
            flops=4 * rows * count * lag_half, bytes_accessed=4 * count * lag_half, transcendentals=0
        ),
        compiler_params=pltpu.CompilerParams(vmem_limit_bytes=GRANT),
    )(slots, *operands)


def mine_kernel(acc_ref, weight_ref, out_ref):
    lay_out(acc_ref, weight_ref, out_ref, 0)


def mine_call(mine, weights):
    rows = mine.shape[0]
    lag_count = mine.shape[1] - LANES
    vmem = pl.BlockSpec(memory_space=pltpu.VMEM)
    return pl.pallas_call(
        mine_kernel,
        in_specs=[vmem] * 2,
        out_specs=vmem,
        out_shape=jax.ShapeDtypeStruct((rows, lag_count), jnp.float32),
        compiler_params=pltpu.CompilerParams(vmem_limit_bytes=GRANT),
        cost_estimate=pl.CostEstimate(
            flops=2 * rows * lag_count * 256, bytes_accessed=8 * rows * lag_count, transcendentals=0
        ),
        name="mine",
    )(mine, weights)


def owner_stacks(spectra, window_mask, pair_slots):
    stations, windows, _, frequency_values = spectra.shape
    slot_count = pair_slots.shape[0]
    half = frequency_values // 2
    lag_half = LAGS // 2
    peers = lax.axis_size("sta")
    me = lax.axis_index("sta")
    core = me & 1
    chip = me >> 1
    core_pairs = [(i, i ^ 1) for i in range(peers)]
    near_pairs = [(i, i ^ 2) for i in range(peers)]
    far_pairs = [(i, (i + 4 - 8 * ((i // 2) % 2)) % peers) for i in range(peers)]
    valid = window_mask.astype(jnp.bfloat16).T[:, None, :, None]
    mark = jnp.broadcast_to(valid, (windows, 2, stations, LANES)).reshape(
        windows, 2 * stations, LANES
    )

    def rows_of(start, size):
        piece = lax.dynamic_slice_in_dim(spectra, start, size, 3)
        return (piece.transpose(1, 2, 0, 3) * valid).reshape(windows, 2 * stations, size)

    splits = [half * cut // 16 for cut in CUTS]
    lead = splits[1]
    own_lead = jnp.concatenate([mark, rows_of(core * half, lead)], axis=2)
    sent = jnp.concatenate([mark, rows_of((1 - core) * half, half)], axis=2)
    par = permute(sent, core_pairs)
    other_slots = permute(pair_slots, core_pairs)
    near = [permute(own_lead, near_pairs), permute(par[:, :, : LANES + lead], near_pairs)]
    own = []
    for at in range(1, len(splits) - 1):
        low, high = splits[at], splits[at + 1]
        own.append(rows_of(core * half + low, high - low))
        piece = jnp.stack([own[-1], par[:, :, LANES + low : LANES + high]])
        if high == half:
            piece, base = lax.optimization_barrier((piece, core * half))
        near.append(permute(piece, near_pairs))
    far = [permute(piece, far_pairs) for piece in near]

    fine = angle_tables(jnp.arange(FINE, dtype=jnp.int32), lag_half, frequency_values)
    coarse = angle_tables(
        base + FINE * jnp.arange(half // FINE, dtype=jnp.int32), lag_half, frequency_values
    )
    slots = jnp.concatenate([pair_slots, other_slots], axis=0)
    slot_chip = slots >> 1
    group = jnp.where(slot_chip == chip, 0, jnp.where(slot_chip == (chip ^ 1), 1, 2))
    other_core = ((slots & 1) != core).astype(jnp.int32)
    live = (slots[:, :1] >= 0).astype(jnp.int32)
    table = jnp.concatenate([group * 2 + other_core, live], axis=1)
    tables = lag_tables(fine, coarse)
    norm = math.sqrt(frequency_values)
    acc = weights = None
    for at in range(len(splits) - 1):
        low, high = splits[at], splits[at + 1]
        last = at == len(splits) - 2
        if at == 0:
            sources = [own_lead, par, near[0], near[1], far[0], far[1]]
            views_at = [(which, None, LANES) for which in range(6)]
        else:
            sources = [own[at - 1], par, near[at + 1], far[at + 1]]
            views_at = [(0, None, 0), (1, None, LANES + low), (2, 0, 0), (2, 1, 0), (3, 0, 0), (3, 1, 0)]
        width = min(SUB, (high - low) // 2)
        made = chunk_call(
            table, sources, views_at, tables, acc, weights, last, low, high - low, width, windows, stations, norm
        )
        if at == 0:
            acc, weights = made
        elif not last:
            (acc,) = made
        else:
            mine, theirs = made
    other = permute(theirs, core_pairs)
    out = (mine_call(mine, weights) + other.astype(jnp.float32)).astype(jnp.bfloat16)
    return out.reshape(slot_count, stations, stations, LAGS)


def solution(mesh):
    placed = (P(("day", "sta"), None, None, None), P(("day", "sta"), None), P("sta", None))
    return jax.shard_map(
        owner_stacks,
        mesh=mesh,
        in_specs=placed,
        out_specs=P(("day", "sta"), None, None, None),
        check_vma=False,
    )
```

```python
import functools
import math

import jax
import jax.numpy as jnp
from jax import lax
from jax.experimental import pallas as pl
from jax.experimental.pallas import tpu as pltpu
from jax.sharding import PartitionSpec as P


LAGS = 1024
CUTS = (0, 8, 12, 16)
SUB = 512
FINE = 64
LANES = 128
GRANT = 24 << 20


def permute(array, pairs):
    return lax.ppermute(array, "sta", pairs)


def angle_tables(index, lag_half, frequency_values):
    lag_index = jnp.arange(1, lag_half + 1, dtype=jnp.int32)
    phase_index = jnp.mod(index[:, None] * lag_index[None, :], 2 * frequency_values)
    phase_angle = phase_index.astype(jnp.float32) * (math.pi / frequency_values)
    return jnp.cos(phase_angle), jnp.sin(phase_angle)


def table_kernel(fine_cos, fine_sin, coarse_cos, coarse_sin, cos_ref, sin_ref):
    fc = fine_cos[...]
    fs = fine_sin[...]

    def one_group(group, carry):
        cc = coarse_cos[pl.ds(group, 1), :]
        cs = coarse_sin[pl.ds(group, 1), :]
        at = pl.ds(pl.multiple_of(group * FINE, FINE), FINE)
        cos_ref[at, :] = (cc * fc - cs * fs).astype(jnp.bfloat16)
        sin_ref[at, :] = (cs * fc + cc * fs).astype(jnp.bfloat16)
        return carry

    lax.fori_loop(0, cos_ref.shape[0] // FINE, one_group, 0)


def lag_tables(fine, coarse):
    count = coarse[0].shape[0] * FINE
    lag_half = fine[0].shape[1]
    vmem = pl.BlockSpec(memory_space=pltpu.VMEM)
    table = jax.ShapeDtypeStruct((count, lag_half), jnp.bfloat16)
    return pl.pallas_call(
        table_kernel,
        in_specs=[vmem] * 4,
        out_specs=[vmem] * 2,
        out_shape=[table, table],
        compiler_params=pltpu.CompilerParams(vmem_limit_bytes=GRANT),
        cost_estimate=pl.CostEstimate(
            flops=6 * count * lag_half, bytes_accessed=4 * count * lag_half, transcendentals=0
        ),
        name="tables",
    )(*fine, *coarse)


def pair_weights(slots_ref, sources, marks, weight_ref, slot_count, windows, stations, norm):
    pairs = stations * stations
    for at, view in enumerate(sources):
        for window in range(windows):
            marks[at, window] = view[window, :, :LANES].astype(jnp.float32)[:stations]
    for slot in range(slot_count):
        first_at = slots_ref[slot, 0]
        second_at = slots_ref[slot, 1]
        live = slots_ref[slot, 2].astype(jnp.float32)
        for station in range(stations):
            count = None
            for window in range(windows):
                term = marks[first_at, window, pl.ds(station, 1), :] * marks[second_at, window]
                count = term if count is None else count + term
            rows = pl.ds(slot * pairs + station * stations, stations)
            weight_ref[rows, :] = live / (norm * jnp.maximum(count, 1.0))


def flip_matrix(size):
    rows_at = lax.broadcasted_iota(jnp.int32, (size, size), 0)
    lanes_at = lax.broadcasted_iota(jnp.int32, (size, size), 1)
    return (rows_at + lanes_at == size - 1).astype(jnp.bfloat16)


def lay_out(acc_ref, weight_ref, out_ref, start):
    rows = out_ref.shape[0]
    lag_half = out_ref.shape[1] // 2
    size = 256
    flip = flip_matrix(size)
    at = pl.ds(start, rows)
    even = acc_ref[at, :lag_half]
    odd = acc_ref[at, lag_half : 2 * lag_half]
    weight = weight_ref[at, :][:, :1]
    still = jnp.sum(acc_ref[at, 2 * lag_half :], axis=1, keepdims=True)
    lane = lax.broadcasted_iota(jnp.int32, (rows, lag_half), 1)
    right = jnp.where(lane == 0, still, pltpu.roll(even - odd, 1, 1))
    out_ref[:, lag_half:] = (right * weight).astype(out_ref.dtype)
    left = (even + odd) * weight
    parts = [left.astype(jnp.bfloat16)]
    if out_ref.dtype == jnp.float32:
        parts.append((left - parts[0].astype(jnp.float32)).astype(jnp.bfloat16))
    for lane in range(0, lag_half, size):
        flipped = sum(
            jnp.dot(part[:, lane : lane + size], flip, preferred_element_type=jnp.float32)
            for part in parts
        )
        out_ref[:, lag_half - lane - size : lag_half - lane] = flipped.astype(out_ref.dtype)


def chunk_kernel(*refs, views_at, slot_count, windows, stations, first, last, low, norm):
    refs = list(refs)
    slots_ref = refs.pop(0)
    sources = [refs.pop(0) for _ in range(1 + max(which for which, _, _ in views_at))]
    cos_ref, sin_ref = (refs.pop(0) for _ in range(2))
    if not first:
        before_ref = refs.pop(0)
    if last:
        weight_ref, mine_ref, theirs_ref = (refs.pop(0) for _ in range(3))
        acc_ref = refs.pop()
    else:
        acc_ref = refs.pop(0)
    if first:
        weight_ref = refs.pop(0)
        marks = refs.pop()
    stage = refs.pop(0)
    buffers = [(refs[0], refs[1]), (refs[2], refs[3])]
    count = stage.shape[-1]
    lag_half = cos_ref.shape[1]
    pairs = stations * stations
    width = buffers[0][0].shape[1]
    wide = 256

    if first:
        pair_weights(slots_ref, sources, marks, weight_ref, slot_count, windows, stations, norm)
        acc_ref[:, 2 * lag_half :] = jnp.zeros((slot_count * pairs, LANES), jnp.float32)
    else:
        acc_ref[:, 2 * lag_half :] = before_ref[:, 2 * lag_half :]

    for at, (which, part, lane) in enumerate(views_at):
        view = sources[which] if part is None else sources[which].at[part]
        for window in range(windows):
            stage[at, window] = view[window, :, lane : lane + count].astype(jnp.float32)

    index = [(slots_ref[slot, 0], slots_ref[slot, 1]) for slot in range(slot_count)]

    def cross(start, real_rows, imag_rows):
        for slot in range(slot_count):
            first_at, second_at = index[slot]
            for tile in range(width // wide):
                lanes = pl.ds(start + tile * wide, wide)
                held = pl.ds(tile * wide, wide)
                second = [
                    [
                        stage[second_at, window, pl.ds(part * stations, stations), lanes]
                        for part in range(2)
                    ]
                    for window in range(windows)
                ]
                for couple in range(0, stations, 2):
                    real_out = []
                    imag_out = []
                    for station in (couple, couple + 1):
                        real = imag = None
                        for window in range(windows):
                            xr = stage[first_at, window, pl.ds(station, 1), lanes]
                            xi = stage[first_at, window, pl.ds(stations + station, 1), lanes]
                            yr, yi = second[window]
                            r = xr * yr + xi * yi
                            i = xi * yr - xr * yi
                            real = r if real is None else real + r
                            imag = i if imag is None else imag + i
                        real_out.append(real)
                        imag_out.append(imag)
                    at = pl.ds(slot * pairs + couple * stations, 2 * stations)
                    real = jnp.concatenate(real_out, axis=0)
                    imag = jnp.concatenate(imag_out, axis=0)
                    real_rows[at, held] = real.astype(jnp.bfloat16)
                    imag_rows[at, held] = imag.astype(jnp.bfloat16)
                    total = real[:, :LANES]
                    for lane in range(LANES, wide, LANES):
                        total = total + real[:, lane : lane + LANES]
                    acc_ref[at, pl.ds(2 * lag_half, LANES)] += total

    def gather_lags(start, real_rows, imag_rows):
        at = pl.ds(low + start, width)
        for lane, rows, table in ((0, real_rows, cos_ref), (lag_half, imag_rows, sin_ref)):
            lanes = slice(lane, lane + lag_half)
            value = jnp.dot(rows[...], table[at, :], preferred_element_type=jnp.float32)
            if start > 0:
                value = value + acc_ref[:, lanes]
            elif not first:
                value = value + before_ref[:, lanes]
            acc_ref[:, lanes] = value

    steps = count // width
    for step in range(steps):
        cross(step * width, *buffers[step % 2])
        if step > 0:
            gather_lags((step - 1) * width, *buffers[(step - 1) % 2])
    gather_lags((steps - 1) * width, *buffers[(steps - 1) % 2])
    if last:
        half = slot_count * pairs // 2
        lay_out(acc_ref, weight_ref, theirs_ref, half)
        mine_ref[...] = acc_ref[:half, :]


def chunk_call(slots, sources, views_at, tables, before, weights, last, low, count, width, windows, stations, norm):
    slot_count = slots.shape[0]
    lag_half = tables[0].shape[1]
    rows = slot_count * stations * stations
    first = before is None
    acc = jax.ShapeDtypeStruct((rows, 2 * lag_half + LANES), jnp.float32)
    operands = list(sources) + list(tables)
    if not first:
        operands.append(before)
    if last:
        operands.append(weights)
    vmem = pl.BlockSpec(memory_space=pltpu.VMEM)
    scratch = [pltpu.VMEM((6, windows, 2 * stations, count), jnp.float32)]
    scratch += [pltpu.VMEM((rows, width), jnp.bfloat16)] * 4
    outs = [acc]
    if first:
        outs.append(jax.ShapeDtypeStruct((rows, LANES), jnp.float32))
        scratch.append(pltpu.VMEM((6, windows, stations, LANES), jnp.float32))
    if last:
        outs = [
            jax.ShapeDtypeStruct((rows // 2, 2 * lag_half + LANES), jnp.float32),
            jax.ShapeDtypeStruct((rows // 2, 2 * lag_half), jnp.bfloat16),
        ]
        scratch.append(pltpu.VMEM(acc.shape, jnp.float32))
    return pl.pallas_call(
        functools.partial(
            chunk_kernel,
            views_at=views_at,
            slot_count=slot_count,
            windows=windows,
            stations=stations,
            first=first,
            last=last,
            low=low,
            norm=norm,
        ),
        in_specs=[pl.BlockSpec(memory_space=pltpu.SMEM)] + [vmem] * len(operands),
        out_specs=[vmem] * len(outs),
        scratch_shapes=scratch,
        out_shape=outs,
        input_output_aliases={} if first or last else {len(operands): 0},
        cost_estimate=pl.CostEstimate(
            flops=4 * rows * count * lag_half, bytes_accessed=4 * count * lag_half, transcendentals=0
        ),
        compiler_params=pltpu.CompilerParams(vmem_limit_bytes=GRANT),
    )(slots, *operands)


def mine_kernel(acc_ref, weight_ref, out_ref):
    lay_out(acc_ref, weight_ref, out_ref, 0)


def mine_call(mine, weights):
    rows = mine.shape[0]
    lag_count = mine.shape[1] - LANES
    vmem = pl.BlockSpec(memory_space=pltpu.VMEM)
    return pl.pallas_call(
        mine_kernel,
        in_specs=[vmem] * 2,
        out_specs=vmem,
        out_shape=jax.ShapeDtypeStruct((rows, lag_count), jnp.float32),
        compiler_params=pltpu.CompilerParams(vmem_limit_bytes=GRANT),
        cost_estimate=pl.CostEstimate(
            flops=2 * rows * lag_count * 256, bytes_accessed=8 * rows * lag_count, transcendentals=0
        ),
        name="mine",
    )(mine, weights)


def owner_stacks(spectra, window_mask, pair_slots):
    stations, windows, _, frequency_values = spectra.shape
    slot_count = pair_slots.shape[0]
    half = frequency_values // 2
    lag_half = LAGS // 2
    peers = lax.axis_size("sta")
    me = lax.axis_index("sta")
    core = me & 1
    chip = me >> 1
    core_pairs = [(i, i ^ 1) for i in range(peers)]
    near_pairs = [(i, i ^ 2) for i in range(peers)]
    far_pairs = [(i, (i + 4 - 8 * ((i // 2) % 2)) % peers) for i in range(peers)]
    split_pairs = dict(far_pairs)
    split_pairs.update({2: 0, peers - 3: peers - 1, 3: peers - 2, peers - 4: 1})
    split_pairs = sorted(split_pairs.items())
    valid = window_mask.astype(jnp.bfloat16).T[:, None, :, None]
    mark = jnp.broadcast_to(valid, (windows, 2, stations, LANES)).reshape(
        windows, 2 * stations, LANES
    )

    def rows_of(start, size):
        piece = lax.dynamic_slice_in_dim(spectra, start, size, 3)
        return (piece.transpose(1, 2, 0, 3) * valid).reshape(windows, 2 * stations, size)

    splits = [half * cut // 16 for cut in CUTS]
    lead = splits[1]
    own_lead = jnp.concatenate([mark, rows_of(core * half, lead)], axis=2)
    sent = jnp.concatenate([mark, rows_of((1 - core) * half, half)], axis=2)
    par = permute(sent, core_pairs)
    other_slots = permute(pair_slots, core_pairs)
    near = [permute(own_lead, near_pairs), permute(par[:, :, : LANES + lead], near_pairs)]
    own = []
    for at in range(1, len(splits) - 1):
        low, high = splits[at], splits[at + 1]
        own.append(rows_of(core * half + low, high - low))
        piece = jnp.stack([own[-1], par[:, :, LANES + low : LANES + high]])
        if high == half:
            piece, base = lax.optimization_barrier((piece, core * half))
        near.append(permute(piece, near_pairs))
    far = [permute(piece, split_pairs if at >= 3 else far_pairs) for at, piece in enumerate(near)]

    fine = angle_tables(jnp.arange(FINE, dtype=jnp.int32), lag_half, frequency_values)
    coarse = angle_tables(
        base + FINE * jnp.arange(half // FINE, dtype=jnp.int32), lag_half, frequency_values
    )
    slots = jnp.concatenate([pair_slots, other_slots], axis=0)
    slot_chip = slots >> 1
    group = jnp.where(slot_chip == chip, 0, jnp.where(slot_chip == (chip ^ 1), 1, 2))
    other_core = ((slots & 1) != core).astype(jnp.int32)
    live = (slots[:, :1] >= 0).astype(jnp.int32)
    table = jnp.concatenate([group * 2 + other_core, live], axis=1)
    tables = lag_tables(fine, coarse)
    norm = math.sqrt(frequency_values)
    acc = weights = None
    units = [(0, 0, lead // 2), (0, lead // 2, lead)]
    units += [(at, splits[at], splits[at + 1]) for at in range(1, len(splits) - 1)]
    for unit, (at, low, high) in enumerate(units):
        last = unit == len(units) - 1
        if at == 0:
            sources = [own_lead, par, near[0], near[1], far[0], far[1]]
            views_at = [(which, None, LANES + low) for which in range(6)]
        else:
            sources = [own[at - 1], par, near[at + 1], far[at + 1]]
            views_at = [(0, None, 0), (1, None, LANES + low), (2, 0, 0), (2, 1, 0), (3, 0, 0), (3, 1, 0)]
        width = SUB // 2 if last else SUB
        made = chunk_call(
            table, sources, views_at, tables, acc, weights, last, low, high - low, width, windows, stations, norm
        )
        if unit == 0:
            acc, weights = made
        elif not last:
            (acc,) = made
        else:
            mine, theirs = made
    other = permute(theirs, core_pairs)
    out = (mine_call(mine, weights) + other.astype(jnp.float32)).astype(jnp.bfloat16)
    return out.reshape(slot_count, stations, stations, LAGS)


def solution(mesh):
    placed = (P(("day", "sta"), None, None, None), P(("day", "sta"), None), P("sta", None))
    return jax.shard_map(
        owner_stacks,
        mesh=mesh,
        in_specs=placed,
        out_specs=P(("day", "sta"), None, None, None),
        check_vma=False,
    )
```

```python
import functools
import math

import jax
import jax.numpy as jnp
from jax import lax
from jax.experimental import pallas as pl
from jax.experimental.pallas import tpu as pltpu
from jax.sharding import PartitionSpec as P


LAGS = 1024
CUTS = (0, 8, 12, 16)
SUB = 512
FINE = 64
LANES = 128
GRANT = 24 << 20


def permute(array, pairs):
    return lax.ppermute(array, "sta", pairs)


def angle_tables(index, lag_half, frequency_values):
    lag_index = jnp.arange(1, lag_half + 1, dtype=jnp.int32)
    phase_index = jnp.mod(index[:, None] * lag_index[None, :], 2 * frequency_values)
    phase_angle = phase_index.astype(jnp.float32) * (math.pi / frequency_values)
    return jnp.cos(phase_angle), jnp.sin(phase_angle)


def table_kernel(fine_cos, fine_sin, coarse_cos, coarse_sin, cos_ref, sin_ref):
    fc = fine_cos[...]
    fs = fine_sin[...]

    def one_group(group, carry):
        cc = coarse_cos[pl.ds(group, 1), :]
        cs = coarse_sin[pl.ds(group, 1), :]
        at = pl.ds(pl.multiple_of(group * FINE, FINE), FINE)
        cos_ref[at, :] = (cc * fc - cs * fs).astype(jnp.bfloat16)
        sin_ref[at, :] = (cs * fc + cc * fs).astype(jnp.bfloat16)
        return carry

    lax.fori_loop(0, cos_ref.shape[0] // FINE, one_group, 0)


def lag_tables(fine, coarse):
    count = coarse[0].shape[0] * FINE
    lag_half = fine[0].shape[1]
    vmem = pl.BlockSpec(memory_space=pltpu.VMEM)
    table = jax.ShapeDtypeStruct((count, lag_half), jnp.bfloat16)
    return pl.pallas_call(
        table_kernel,
        in_specs=[vmem] * 4,
        out_specs=[vmem] * 2,
        out_shape=[table, table],
        compiler_params=pltpu.CompilerParams(vmem_limit_bytes=GRANT),
        cost_estimate=pl.CostEstimate(
            flops=6 * count * lag_half, bytes_accessed=4 * count * lag_half, transcendentals=0
        ),
        name="tables",
    )(*fine, *coarse)


def pair_weights(slots_ref, sources, marks, weight_ref, slot_count, windows, stations, norm):
    pairs = stations * stations
    own_mark, par, near, far = sources
    views = [(own_mark, 0), (par, 0), (near, 0), (near, 1), (far, 0), (far, 1)]
    for at, (view, part) in enumerate(views):
        for window in range(windows):
            mark = view[window, :, :LANES].astype(jnp.float32)
            marks[at, window] = mark[part * stations : (part + 1) * stations]
    for slot in range(slot_count):
        first_at = slots_ref[slot, 0]
        second_at = slots_ref[slot, 1]
        live = slots_ref[slot, 2].astype(jnp.float32)
        for station in range(stations):
            count = None
            for window in range(windows):
                term = marks[first_at, window, pl.ds(station, 1), :] * marks[second_at, window]
                count = term if count is None else count + term
            rows = pl.ds(slot * pairs + station * stations, stations)
            weight_ref[rows, :] = live / (norm * jnp.maximum(count, 1.0))


def flip_matrix(size):
    rows_at = lax.broadcasted_iota(jnp.int32, (size, size), 0)
    lanes_at = lax.broadcasted_iota(jnp.int32, (size, size), 1)
    return (rows_at + lanes_at == size - 1).astype(jnp.bfloat16)


def lay_out(acc_ref, weight_ref, out_ref, start):
    rows = out_ref.shape[0]
    lag_half = out_ref.shape[1] // 2
    size = 256
    flip = flip_matrix(size)
    at = pl.ds(start, rows)
    even = acc_ref[at, :lag_half]
    odd = acc_ref[at, lag_half : 2 * lag_half]
    weight = weight_ref[at, :][:, :1]
    still = jnp.sum(acc_ref[at, 2 * lag_half :], axis=1, keepdims=True)
    lane = lax.broadcasted_iota(jnp.int32, (rows, lag_half), 1)
    right = jnp.where(lane == 0, still, pltpu.roll(even - odd, 1, 1))
    out_ref[:, lag_half:] = (right * weight).astype(out_ref.dtype)
    left = (even + odd) * weight
    parts = [left.astype(jnp.bfloat16)]
    if out_ref.dtype == jnp.float32:
        parts.append((left - parts[0].astype(jnp.float32)).astype(jnp.bfloat16))
    for lane in range(0, lag_half, size):
        flipped = sum(
            jnp.dot(part[:, lane : lane + size], flip, preferred_element_type=jnp.float32)
            for part in parts
        )
        out_ref[:, lag_half - lane - size : lag_half - lane] = flipped.astype(out_ref.dtype)


def chunk_kernel(*refs, views_at, slot_count, windows, stations, first, last, low, norm):
    refs = list(refs)
    slots_ref = refs.pop(0)
    sources = [refs.pop(0) for _ in range(1 + max(which for which, _, _ in views_at))]
    mark_source = refs.pop(0)
    cos_ref, sin_ref = (refs.pop(0) for _ in range(2))
    if not first:
        before_ref = refs.pop(0)
    if last:
        weight_ref, mine_ref, theirs_ref = (refs.pop(0) for _ in range(3))
        acc_ref = refs.pop()
    else:
        acc_ref = refs.pop(0)
    if first:
        weight_ref = refs.pop(0)
        marks = refs.pop(0)
    stage = refs.pop(0)
    buffers = [(refs[0], refs[1]), (refs[2], refs[3])]
    count = stage.shape[-1]
    lag_half = cos_ref.shape[1]
    pairs = stations * stations
    width = buffers[0][0].shape[1]
    wide = 256

    if not first:
        marks = mark_source
    if first:
        pair_weights(slots_ref, [mark_source, sources[1], sources[3], sources[5]], marks, weight_ref, slot_count, windows, stations, norm)
        acc_ref[:, 2 * lag_half :] = jnp.zeros((slot_count * pairs, LANES), jnp.float32)
    else:
        acc_ref[:, 2 * lag_half :] = before_ref[:, 2 * lag_half :]

    for at, (which, part, lane) in enumerate(views_at):
        view = sources[which] if part is None else sources[which].at[part]
        for window in range(windows):
            mark = marks[at, window]
            mark = jnp.concatenate([mark, mark], axis=0)
            for start in range(0, count, LANES):
                piece = view[window, :, lane + start : lane + start + LANES]
                stage[at, window, :, start : start + LANES] = piece.astype(jnp.float32) * mark

    index = [(slots_ref[slot, 0], slots_ref[slot, 1]) for slot in range(slot_count)]

    def cross(start, real_rows, imag_rows):
        for slot in range(slot_count):
            first_at, second_at = index[slot]
            for tile in range(width // wide):
                lanes = pl.ds(start + tile * wide, wide)
                held = pl.ds(tile * wide, wide)
                second = [
                    [
                        stage[second_at, window, pl.ds(part * stations, stations), lanes]
                        for part in range(2)
                    ]
                    for window in range(windows)
                ]
                for couple in range(0, stations, 2):
                    real_out = []
                    imag_out = []
                    for station in (couple, couple + 1):
                        real = imag = None
                        for window in range(windows):
                            xr = stage[first_at, window, pl.ds(station, 1), lanes]
                            xi = stage[first_at, window, pl.ds(stations + station, 1), lanes]
                            yr, yi = second[window]
                            r = xr * yr + xi * yi
                            i = xi * yr - xr * yi
                            real = r if real is None else real + r
                            imag = i if imag is None else imag + i
                        real_out.append(real)
                        imag_out.append(imag)
                    at = pl.ds(slot * pairs + couple * stations, 2 * stations)
                    real = jnp.concatenate(real_out, axis=0)
                    imag = jnp.concatenate(imag_out, axis=0)
                    real_rows[at, held] = real.astype(jnp.bfloat16)
                    imag_rows[at, held] = imag.astype(jnp.bfloat16)
                    total = real[:, :LANES]
                    for lane in range(LANES, wide, LANES):
                        total = total + real[:, lane : lane + LANES]
                    acc_ref[at, pl.ds(2 * lag_half, LANES)] += total

    def gather_lags(start, real_rows, imag_rows):
        at = pl.ds(low + start, width)
        for lane, rows, table in ((0, real_rows, cos_ref), (lag_half, imag_rows, sin_ref)):
            lanes = slice(lane, lane + lag_half)
            value = jnp.dot(rows[...], table[at, :], preferred_element_type=jnp.float32)
            if start > 0:
                value = value + acc_ref[:, lanes]
            elif not first:
                value = value + before_ref[:, lanes]
            acc_ref[:, lanes] = value

    steps = count // width
    for step in range(steps):
        cross(step * width, *buffers[step % 2])
        if step > 0:
            gather_lags((step - 1) * width, *buffers[(step - 1) % 2])
    gather_lags((steps - 1) * width, *buffers[(steps - 1) % 2])
    if last:
        half = slot_count * pairs // 2
        lay_out(acc_ref, weight_ref, theirs_ref, half)
        mine_ref[...] = acc_ref[:half, :]


def chunk_call(slots, sources, views_at, mark_source, tables, before, weights, last, low, count, width, windows, stations, norm):
    slot_count = slots.shape[0]
    lag_half = tables[0].shape[1]
    rows = slot_count * stations * stations
    first = before is None
    acc = jax.ShapeDtypeStruct((rows, 2 * lag_half + LANES), jnp.float32)
    operands = list(sources) + [mark_source] + list(tables)
    if not first:
        operands.append(before)
    if last:
        operands.append(weights)
    vmem = pl.BlockSpec(memory_space=pltpu.VMEM)
    scratch = [pltpu.VMEM((6, windows, 2 * stations, count), jnp.float32)]
    scratch += [pltpu.VMEM((rows, width), jnp.bfloat16)] * 4
    outs = [acc]
    if first:
        outs.append(jax.ShapeDtypeStruct((rows, LANES), jnp.float32))
        outs.append(jax.ShapeDtypeStruct((6, windows, stations, LANES), jnp.float32))
    if last:
        outs = [
            jax.ShapeDtypeStruct((rows // 2, 2 * lag_half + LANES), jnp.float32),
            jax.ShapeDtypeStruct((rows // 2, 2 * lag_half), jnp.bfloat16),
        ]
        scratch.append(pltpu.VMEM(acc.shape, jnp.float32))
    return pl.pallas_call(
        functools.partial(
            chunk_kernel,
            views_at=views_at,
            slot_count=slot_count,
            windows=windows,
            stations=stations,
            first=first,
            last=last,
            low=low,
            norm=norm,
        ),
        in_specs=[pl.BlockSpec(memory_space=pltpu.SMEM)] + [vmem] * len(operands),
        out_specs=[vmem] * len(outs),
        scratch_shapes=scratch,
        out_shape=outs,
        input_output_aliases={} if first or last else {len(operands): 0},
        cost_estimate=pl.CostEstimate(
            flops=4 * rows * count * lag_half, bytes_accessed=4 * count * lag_half, transcendentals=0
        ),
        compiler_params=pltpu.CompilerParams(vmem_limit_bytes=GRANT),
    )(slots, *operands)


def mine_kernel(acc_ref, weight_ref, out_ref):
    lay_out(acc_ref, weight_ref, out_ref, 0)


def mine_call(mine, weights):
    rows = mine.shape[0]
    lag_count = mine.shape[1] - LANES
    vmem = pl.BlockSpec(memory_space=pltpu.VMEM)
    return pl.pallas_call(
        mine_kernel,
        in_specs=[vmem] * 2,
        out_specs=vmem,
        out_shape=jax.ShapeDtypeStruct((rows, lag_count), jnp.float32),
        compiler_params=pltpu.CompilerParams(vmem_limit_bytes=GRANT),
        cost_estimate=pl.CostEstimate(
            flops=2 * rows * lag_count * 256, bytes_accessed=8 * rows * lag_count, transcendentals=0
        ),
        name="mine",
    )(mine, weights)


def owner_stacks(spectra, window_mask, pair_slots):
    stations, windows, _, frequency_values = spectra.shape
    slot_count = pair_slots.shape[0]
    half = frequency_values // 2
    lag_half = LAGS // 2
    peers = lax.axis_size("sta")
    me = lax.axis_index("sta")
    core = me & 1
    chip = me >> 1
    core_pairs = [(i, i ^ 1) for i in range(peers)]
    near_pairs = [(i, i ^ 2) for i in range(peers)]
    far_pairs = [(i, (i + 4 - 8 * ((i // 2) % 2)) % peers) for i in range(peers)]
    split_pairs = dict(far_pairs)
    split_pairs.update({2: 0, peers - 3: peers - 1, 3: peers - 2, peers - 4: 1})
    split_pairs = sorted(split_pairs.items())
    unit_scale = lax.optimization_barrier(jnp.ones((), jnp.bfloat16))

    def rows_of(start, size):
        piece = lax.dynamic_slice_in_dim(spectra, start, size, 3)
        return (piece.transpose(1, 2, 0, 3) * unit_scale).reshape(windows, 2 * stations, size)

    splits = [half * cut // 16 for cut in CUTS]
    lead = splits[1]
    own_lead = rows_of(core * half, lead)
    valid = window_mask.astype(jnp.bfloat16).T[:, None, :, None]
    mark = jnp.broadcast_to(valid, (windows, 2, stations, LANES)).reshape(
        windows, 2 * stations, LANES
    )
    sent = jnp.concatenate([mark, rows_of((1 - core) * half, half)], axis=2)
    par = permute(sent, core_pairs)
    both = jnp.concatenate([mark[:, :stations], par[:, :stations, :LANES]], axis=1)
    par_lead = jnp.concatenate([both, par[:, :, LANES : LANES + lead]], axis=2)
    other_slots = permute(pair_slots, core_pairs)
    near = [permute(own_lead, near_pairs), permute(par_lead, near_pairs)]
    own = []
    for at in range(1, len(splits) - 1):
        low, high = splits[at], splits[at + 1]
        own.append(rows_of(core * half + low, high - low))
        piece = jnp.stack([own[-1], par[:, :, LANES + low : LANES + high]])
        if high == half:
            piece, base = lax.optimization_barrier((piece, core * half))
        near.append(permute(piece, near_pairs))
    far = [permute(piece, split_pairs if at >= 3 else far_pairs) for at, piece in enumerate(near)]

    fine = angle_tables(jnp.arange(FINE, dtype=jnp.int32), lag_half, frequency_values)
    coarse = angle_tables(
        base + FINE * jnp.arange(half // FINE, dtype=jnp.int32), lag_half, frequency_values
    )
    slots = jnp.concatenate([pair_slots, other_slots], axis=0)
    slot_chip = slots >> 1
    group = jnp.where(slot_chip == chip, 0, jnp.where(slot_chip == (chip ^ 1), 1, 2))
    other_core = ((slots & 1) != core).astype(jnp.int32)
    live = (slots[:, :1] >= 0).astype(jnp.int32)
    table = jnp.concatenate([group * 2 + other_core, live], axis=1)
    tables = lag_tables(fine, coarse)
    norm = math.sqrt(frequency_values)
    acc = weights = None
    units = [(0, 0, lead // 512 * 256), (0, lead // 512 * 256, lead)]
    mark_source = mark
    units += [(at, splits[at], splits[at + 1]) for at in range(1, len(splits) - 1)]
    for unit, (at, low, high) in enumerate(units):
        last = unit == len(units) - 1
        if at == 0:
            sources = [own_lead, par, near[0], near[1], far[0], far[1]]
            views_at = [(which, None, low + LANES * (which in (1, 3, 5))) for which in range(6)]
        else:
            sources = [own[at - 1], par, near[at + 1], far[at + 1]]
            views_at = [(0, None, 0), (1, None, LANES + low), (2, 0, 0), (2, 1, 0), (3, 0, 0), (3, 1, 0)]
        width = SUB // 2 if last or (high - low) % SUB else SUB
        made = chunk_call(
            table, sources, views_at, mark_source, tables, acc, weights, last, low, high - low, width, windows, stations, norm
        )
        if unit == 0:
            acc, weights, mark_source = made
        elif not last:
            (acc,) = made
        else:
            mine, theirs = made
    other = permute(theirs, core_pairs)
    out = (mine_call(mine, weights) + other.astype(jnp.float32)).astype(jnp.bfloat16)
    return out.reshape(slot_count, stations, stations, LAGS)


def solution(mesh):
    placed = (P(("day", "sta"), None, None, None), P(("day", "sta"), None), P("sta", None))
    return jax.shard_map(
        owner_stacks,
        mesh=mesh,
        in_specs=placed,
        out_specs=P(("day", "sta"), None, None, None),
        check_vma=False,
    )
```

```python
import functools
import math

import jax
import jax.numpy as jnp
from jax import lax
from jax.experimental import pallas as pl
from jax.experimental.pallas import tpu as pltpu
from jax.sharding import PartitionSpec as P


LAGS = 1024
CUTS = (0, 8, 12, 16)
SUB = 512
FINE = 64
LANES = 128
GRANT = 24 << 20


def permute(array, pairs):
    return lax.ppermute(array, "sta", pairs)


def angle_tables(index, lag_half, frequency_values):
    lag_index = jnp.arange(1, lag_half + 1, dtype=jnp.int32)
    phase_index = jnp.mod(index[:, None] * lag_index[None, :], 2 * frequency_values)
    phase_angle = phase_index.astype(jnp.float32) * (math.pi / frequency_values)
    return jnp.cos(phase_angle), jnp.sin(phase_angle)


def table_kernel(fine_cos, fine_sin, coarse_cos, coarse_sin, cos_ref, sin_ref):
    fc = fine_cos[...]
    fs = fine_sin[...]

    def one_group(group, carry):
        cc = coarse_cos[pl.ds(group, 1), :]
        cs = coarse_sin[pl.ds(group, 1), :]
        at = pl.ds(pl.multiple_of(group * FINE, FINE), FINE)
        cos_ref[at, :] = (cc * fc - cs * fs).astype(jnp.bfloat16)
        sin_ref[at, :] = (cs * fc + cc * fs).astype(jnp.bfloat16)
        return carry

    lax.fori_loop(0, cos_ref.shape[0] // FINE, one_group, 0)


def lag_tables(fine, coarse):
    count = coarse[0].shape[0] * FINE
    lag_half = fine[0].shape[1]
    vmem = pl.BlockSpec(memory_space=pltpu.VMEM)
    table = jax.ShapeDtypeStruct((count, lag_half), jnp.bfloat16)
    return pl.pallas_call(
        table_kernel,
        in_specs=[vmem] * 4,
        out_specs=[vmem] * 2,
        out_shape=[table, table],
        compiler_params=pltpu.CompilerParams(vmem_limit_bytes=GRANT),
        cost_estimate=pl.CostEstimate(
            flops=6 * count * lag_half, bytes_accessed=4 * count * lag_half, transcendentals=0
        ),
        name="tables",
    )(*fine, *coarse)


def pair_weights(slots_ref, sources, marks, weight_ref, slot_count, windows, stations, norm):
    pairs = stations * stations
    own_mark, par, near, far = sources
    views = [(own_mark, 0), (par, 0), (near, 0), (near, 1), (far, 0), (far, 1)]
    for at, (view, part) in enumerate(views):
        for window in range(windows):
            mark = view[window, :, :LANES].astype(jnp.float32)
            marks[at, window] = mark[part * stations : (part + 1) * stations]
    for slot in range(slot_count):
        first_at = slots_ref[slot, 0]
        second_at = slots_ref[slot, 1]
        live = slots_ref[slot, 2].astype(jnp.float32)
        for station in range(stations):
            count = None
            for window in range(windows):
                term = marks[first_at, window, pl.ds(station, 1), :] * marks[second_at, window]
                count = term if count is None else count + term
            rows = pl.ds(slot * pairs + station * stations, stations)
            weight_ref[rows, :] = live / (norm * jnp.maximum(count, 1.0))


def flip_matrix(size):
    rows_at = lax.broadcasted_iota(jnp.int32, (size, size), 0)
    lanes_at = lax.broadcasted_iota(jnp.int32, (size, size), 1)
    return (rows_at + lanes_at == size - 1).astype(jnp.bfloat16)


def lay_out(acc_ref, weight_ref, out_ref, start):
    rows = out_ref.shape[0]
    lag_half = out_ref.shape[1] // 2
    size = 256
    flip = flip_matrix(size)
    even = acc_ref[:, :lag_half]
    odd = acc_ref[:, lag_half : 2 * lag_half]
    weight = weight_ref[start : start + rows, :][:, :1]
    still = jnp.sum(acc_ref[:, 2 * lag_half :], axis=1, keepdims=True)
    lane = lax.broadcasted_iota(jnp.int32, (rows, lag_half), 1)
    right = jnp.where(lane == 0, still, pltpu.roll(even - odd, 1, 1))
    out_ref[:, lag_half:] = (right * weight).astype(out_ref.dtype)
    left = (even + odd) * weight
    parts = [left.astype(jnp.bfloat16)]
    if out_ref.dtype == jnp.float32:
        parts.append((left - parts[0].astype(jnp.float32)).astype(jnp.bfloat16))
    for lane in range(0, lag_half, size):
        flipped = sum(
            jnp.dot(part[:, lane : lane + size], flip, preferred_element_type=jnp.float32)
            for part in parts
        )
        out_ref[:, lag_half - lane - size : lag_half - lane] = flipped.astype(out_ref.dtype)


def chunk_kernel(*refs, views_at, slot_count, slot_base, windows, stations, first, last, low, norm):
    refs = list(refs)
    slots_ref = refs.pop(0)
    sources = [refs.pop(0) for _ in range(1 + max(which for which, _, _ in views_at))]
    mark_source = refs.pop(0)
    cos_ref, sin_ref = (refs.pop(0) for _ in range(2))
    if not first:
        before_ref = refs.pop(0)
    if last:
        weight_ref, out_ref = (refs.pop(0) for _ in range(2))
        acc_ref = refs.pop()
    else:
        acc_ref = refs.pop(0)
    if first:
        weight_ref = refs.pop(0)
        marks = refs.pop(0)
    stage = refs.pop(0)
    buffers = [(refs[0], refs[1]), (refs[2], refs[3])]
    count = stage.shape[-1]
    lag_half = cos_ref.shape[1]
    pairs = stations * stations
    width = buffers[0][0].shape[1]
    wide = 256
    held_rows = slice(slot_base * pairs, (slot_base + slot_count) * pairs)

    if not first:
        marks = mark_source
    if first:
        pair_weights(slots_ref, [mark_source, sources[1], sources[3], sources[5]], marks, weight_ref, slot_count, windows, stations, norm)
        acc_ref[:, 2 * lag_half :] = jnp.zeros((slot_count * pairs, LANES), jnp.float32)
    else:
        acc_ref[:, 2 * lag_half :] = before_ref[held_rows, 2 * lag_half :]

    for at, (which, part, lane) in enumerate(views_at):
        view = sources[which] if part is None else sources[which].at[part]
        for window in range(windows):
            mark = marks[at, window]
            mark = jnp.concatenate([mark, mark], axis=0)
            for start in range(0, count, LANES):
                piece = view[window, :, lane + start : lane + start + LANES]
                stage[at, window, :, start : start + LANES] = piece.astype(jnp.float32) * mark

    index = [(slots_ref[slot_base + slot, 0], slots_ref[slot_base + slot, 1]) for slot in range(slot_count)]

    def cross(start, real_rows, imag_rows):
        for slot in range(slot_count):
            first_at, second_at = index[slot]
            for tile in range(width // wide):
                lanes = pl.ds(start + tile * wide, wide)
                held = pl.ds(tile * wide, wide)
                second = [
                    [
                        stage[second_at, window, pl.ds(part * stations, stations), lanes]
                        for part in range(2)
                    ]
                    for window in range(windows)
                ]
                for couple in range(0, stations, 2):
                    real_out = []
                    imag_out = []
                    for station in (couple, couple + 1):
                        real = imag = None
                        for window in range(windows):
                            xr = stage[first_at, window, pl.ds(station, 1), lanes]
                            xi = stage[first_at, window, pl.ds(stations + station, 1), lanes]
                            yr, yi = second[window]
                            r = xr * yr + xi * yi
                            i = xi * yr - xr * yi
                            real = r if real is None else real + r
                            imag = i if imag is None else imag + i
                        real_out.append(real)
                        imag_out.append(imag)
                    at = pl.ds(slot * pairs + couple * stations, 2 * stations)
                    real = jnp.concatenate(real_out, axis=0)
                    imag = jnp.concatenate(imag_out, axis=0)
                    real_rows[at, held] = real.astype(jnp.bfloat16)
                    imag_rows[at, held] = imag.astype(jnp.bfloat16)
                    total = real[:, :LANES]
                    for lane in range(LANES, wide, LANES):
                        total = total + real[:, lane : lane + LANES]
                    acc_ref[at, pl.ds(2 * lag_half, LANES)] += total

    def gather_lags(start, real_rows, imag_rows):
        at = pl.ds(low + start, width)
        for lane, rows, table in ((0, real_rows, cos_ref), (lag_half, imag_rows, sin_ref)):
            lanes = slice(lane, lane + lag_half)
            value = jnp.dot(rows[...], table[at, :], preferred_element_type=jnp.float32)
            if start > 0:
                value = value + acc_ref[:, lanes]
            elif not first:
                value = value + before_ref[held_rows, lanes]
            acc_ref[:, lanes] = value

    steps = count // width
    for step in range(steps):
        cross(step * width, *buffers[step % 2])
        if step > 0:
            gather_lags((step - 1) * width, *buffers[(step - 1) % 2])
    gather_lags((steps - 1) * width, *buffers[(steps - 1) % 2])
    if last:
        lay_out(acc_ref, weight_ref, out_ref, slot_base * pairs)


def chunk_call(slots, sources, views_at, mark_source, tables, before, weights, last, slot_base, slot_count, low, count, width, windows, stations, norm):
    lag_half = tables[0].shape[1]
    rows = slot_count * stations * stations
    first = before is None
    acc = jax.ShapeDtypeStruct((rows, 2 * lag_half + LANES), jnp.float32)
    operands = list(sources) + [mark_source] + list(tables)
    if not first:
        operands.append(before)
    if last:
        operands.append(weights)
    vmem = pl.BlockSpec(memory_space=pltpu.VMEM)
    scratch = [pltpu.VMEM((6, windows, 2 * stations, count), jnp.float32)]
    scratch += [pltpu.VMEM((rows, width), jnp.bfloat16)] * 4
    outs = [acc]
    if first:
        outs.append(jax.ShapeDtypeStruct((rows, LANES), jnp.float32))
        outs.append(jax.ShapeDtypeStruct((6, windows, stations, LANES), jnp.float32))
    if last:
        outs = [jax.ShapeDtypeStruct((rows, 2 * lag_half), last)]
        scratch.append(pltpu.VMEM(acc.shape, jnp.float32))
    return pl.pallas_call(
        functools.partial(
            chunk_kernel,
            views_at=views_at,
            slot_count=slot_count,
            slot_base=slot_base,
            windows=windows,
            stations=stations,
            first=first,
            last=last,
            low=low,
            norm=norm,
        ),
        in_specs=[pl.BlockSpec(memory_space=pltpu.SMEM)] + [vmem] * len(operands),
        out_specs=[vmem] * len(outs),
        scratch_shapes=scratch,
        out_shape=outs,
        input_output_aliases={} if first or last else {len(operands): 0},
        cost_estimate=pl.CostEstimate(
            flops=4 * rows * count * lag_half, bytes_accessed=4 * count * lag_half, transcendentals=0
        ),
        compiler_params=pltpu.CompilerParams(vmem_limit_bytes=GRANT),
    )(slots, *operands)


def owner_stacks(spectra, window_mask, pair_slots):
    stations, windows, _, frequency_values = spectra.shape
    slot_count = pair_slots.shape[0]
    half = frequency_values // 2
    lag_half = LAGS // 2
    peers = lax.axis_size("sta")
    me = lax.axis_index("sta")
    core = me & 1
    chip = me >> 1
    core_pairs = [(i, i ^ 1) for i in range(peers)]
    near_pairs = [(i, i ^ 2) for i in range(peers)]
    far_pairs = [(i, (i + 4 - 8 * ((i // 2) % 2)) % peers) for i in range(peers)]
    split_pairs = dict(far_pairs)
    split_pairs.update({2: 0, peers - 3: peers - 1, 3: peers - 2, peers - 4: 1})
    split_pairs = sorted(split_pairs.items())
    unit_scale = lax.optimization_barrier(jnp.ones((), jnp.bfloat16))

    def rows_of(start, size):
        piece = lax.dynamic_slice_in_dim(spectra, start, size, 3)
        return (piece.transpose(1, 2, 0, 3) * unit_scale).reshape(windows, 2 * stations, size)

    splits = [half * cut // 16 for cut in CUTS]
    lead = splits[1]
    own_lead = rows_of(core * half, lead)
    valid = window_mask.astype(jnp.bfloat16).T[:, None, :, None]
    mark = jnp.broadcast_to(valid, (windows, 2, stations, LANES)).reshape(
        windows, 2 * stations, LANES
    )
    sent = jnp.concatenate([mark, rows_of((1 - core) * half, half)], axis=2)
    par = permute(sent, core_pairs)
    both = jnp.concatenate([mark[:, :stations], par[:, :stations, :LANES]], axis=1)
    par_lead = jnp.concatenate([both, par[:, :, LANES : LANES + lead]], axis=2)
    other_slots = permute(pair_slots, core_pairs)
    near = [permute(own_lead, near_pairs), permute(par_lead, near_pairs)]
    own = []
    for at in range(1, len(splits) - 1):
        low, high = splits[at], splits[at + 1]
        own.append(rows_of(core * half + low, high - low))
        piece = jnp.stack([own[-1], par[:, :, LANES + low : LANES + high]])
        if high == half:
            piece, base = lax.optimization_barrier((piece, core * half))
        near.append(permute(piece, near_pairs))
    far = [permute(piece, split_pairs if at >= 3 else far_pairs) for at, piece in enumerate(near)]

    fine = angle_tables(jnp.arange(FINE, dtype=jnp.int32), lag_half, frequency_values)
    coarse = angle_tables(
        base + FINE * jnp.arange(half // FINE, dtype=jnp.int32), lag_half, frequency_values
    )
    slots = jnp.concatenate([pair_slots, other_slots], axis=0)
    slot_chip = slots >> 1
    group = jnp.where(slot_chip == chip, 0, jnp.where(slot_chip == (chip ^ 1), 1, 2))
    other_core = ((slots & 1) != core).astype(jnp.int32)
    live = (slots[:, :1] >= 0).astype(jnp.int32)
    table = jnp.concatenate([group * 2 + other_core, live], axis=1)
    tables = lag_tables(fine, coarse)
    norm = math.sqrt(frequency_values)
    acc = weights = None
    units = [(0, 0, lead // 512 * 256), (0, lead // 512 * 256, lead)]
    mark_source = mark
    units += [(at, splits[at], splits[at + 1]) for at in range(1, len(splits) - 1)]
    for unit, (at, low, high) in enumerate(units):
        last = unit == len(units) - 1
        if at == 0:
            sources = [own_lead, par, near[0], near[1], far[0], far[1]]
            views_at = [(which, None, low + LANES * (which in (1, 3, 5))) for which in range(6)]
        else:
            sources = [own[at - 1], par, near[at + 1], far[at + 1]]
            views_at = [(0, None, 0), (1, None, LANES + low), (2, 0, 0), (2, 1, 0), (3, 0, 0), (3, 1, 0)]
        width = SUB // 2 if last or (high - low) % SUB else SUB

        def part(kind, slot_base, slots_here):
            return chunk_call(
                table, sources, views_at, mark_source, tables, acc, weights, kind,
                slot_base, slots_here, low, high - low, width, windows, stations, norm,
            )

        if last:
            (theirs,) = part(jnp.bfloat16, slot_count, slot_count)
            other = permute(theirs, core_pairs)
            (mine,) = part(jnp.float32, 0, slot_count)
        elif unit == 0:
            acc, weights, mark_source = part(None, 0, 2 * slot_count)
        else:
            (acc,) = part(None, 0, 2 * slot_count)
    out = (mine + other.astype(jnp.float32)).astype(jnp.bfloat16)
    return out.reshape(slot_count, stations, stations, LAGS)


def solution(mesh):
    placed = (P(("day", "sta"), None, None, None), P(("day", "sta"), None), P("sta", None))
    return jax.shard_map(
        owner_stacks,
        mesh=mesh,
        in_specs=placed,
        out_specs=P(("day", "sta"), None, None, None),
        check_vma=False,
    )
```

```python
import functools
import math

import jax
import jax.numpy as jnp
from jax import lax
from jax.experimental import pallas as pl
from jax.experimental.pallas import tpu as pltpu
from jax.sharding import PartitionSpec as P


LAGS = 1024
CUTS = (0, 8, 12, 16)
SUB = 512
FINE = 64
LANES = 128
GRANT = 24 << 20


def permute(array, pairs):
    return lax.ppermute(array, "sta", pairs)


def angle_tables(index, lag_half, frequency_values):
    lag_index = jnp.arange(1, lag_half + 1, dtype=jnp.int32)
    phase_index = jnp.mod(index[:, None] * lag_index[None, :], 2 * frequency_values)
    phase_angle = phase_index.astype(jnp.float32) * (math.pi / frequency_values)
    return jnp.cos(phase_angle), jnp.sin(phase_angle)


def table_kernel(fine_cos, fine_sin, coarse_cos, coarse_sin, cos_ref, sin_ref):
    fc = fine_cos[...]
    fs = fine_sin[...]

    def one_group(group, carry):
        cc = coarse_cos[pl.ds(group, 1), :]
        cs = coarse_sin[pl.ds(group, 1), :]
        at = pl.ds(pl.multiple_of(group * FINE, FINE), FINE)
        cos_ref[at, :] = (cc * fc - cs * fs).astype(jnp.bfloat16)
        sin_ref[at, :] = (cs * fc + cc * fs).astype(jnp.bfloat16)
        return carry

    lax.fori_loop(0, cos_ref.shape[0] // FINE, one_group, 0)


def lag_tables(fine, coarse):
    count = coarse[0].shape[0] * FINE
    lag_half = fine[0].shape[1]
    vmem = pl.BlockSpec(memory_space=pltpu.VMEM)
    table = jax.ShapeDtypeStruct((count, lag_half), jnp.bfloat16)
    return pl.pallas_call(
        table_kernel,
        in_specs=[vmem] * 4,
        out_specs=[vmem] * 2,
        out_shape=[table, table],
        compiler_params=pltpu.CompilerParams(vmem_limit_bytes=GRANT),
        cost_estimate=pl.CostEstimate(
            flops=6 * count * lag_half, bytes_accessed=4 * count * lag_half, transcendentals=0
        ),
        name="tables",
    )(*fine, *coarse)


def pair_weights(slots_ref, sources, marks, weight_ref, slot_count, windows, stations, norm):
    pairs = stations * stations
    own_mark, par, near, far = sources
    views = [(own_mark, 0), (par, 0), (near, 0), (near, 1), (far, 0), (far, 1)]
    for at, (view, part) in enumerate(views):
        for window in range(windows):
            mark = view[window, :, :LANES].astype(jnp.float32)
            marks[at, window] = mark[part * stations : (part + 1) * stations]
    for slot in range(slot_count):
        first_at = slots_ref[slot, 0]
        second_at = slots_ref[slot, 1]
        live = slots_ref[slot, 2].astype(jnp.float32)
        for station in range(stations):
            count = None
            for window in range(windows):
                term = marks[first_at, window, pl.ds(station, 1), :] * marks[second_at, window]
                count = term if count is None else count + term
            rows = pl.ds(slot * pairs + station * stations, stations)
            weight_ref[rows, :] = live / (norm * jnp.maximum(count, 1.0))


def flip_matrix(size):
    rows_at = lax.broadcasted_iota(jnp.int32, (size, size), 0)
    lanes_at = lax.broadcasted_iota(jnp.int32, (size, size), 1)
    return (rows_at + lanes_at == size - 1).astype(jnp.bfloat16)


def lay_out(acc_ref, weight_ref, out_ref, start):
    rows = out_ref.shape[0]
    lag_half = out_ref.shape[1] // 2
    size = 256
    flip = flip_matrix(size)
    even = acc_ref[:, :lag_half]
    odd = acc_ref[:, lag_half : 2 * lag_half]
    weight = weight_ref[start : start + rows, :][:, :1]
    still = jnp.sum(acc_ref[:, 2 * lag_half :], axis=1, keepdims=True)
    lane = lax.broadcasted_iota(jnp.int32, (rows, lag_half), 1)
    right = jnp.where(lane == 0, still, pltpu.roll(even - odd, 1, 1))
    out_ref[:, lag_half:] = (right * weight).astype(out_ref.dtype)
    left = (even + odd) * weight
    parts = [left.astype(jnp.bfloat16)]
    if out_ref.dtype == jnp.float32:
        parts.append((left - parts[0].astype(jnp.float32)).astype(jnp.bfloat16))
    for lane in range(0, lag_half, size):
        flipped = sum(
            jnp.dot(part[:, lane : lane + size], flip, preferred_element_type=jnp.float32)
            for part in parts
        )
        out_ref[:, lag_half - lane - size : lag_half - lane] = flipped.astype(out_ref.dtype)


def chunk_kernel(*refs, views_at, slot_count, slot_base, windows, stations, first, last, low, norm, staged):
    refs = list(refs)
    slots_ref = refs.pop(0)
    sources = [refs.pop(0) for _ in range(0 if staged else 1 + max(which for which, _, _ in views_at))]
    mark_source = refs.pop(0)
    cos_ref, sin_ref = (refs.pop(0) for _ in range(2))
    if not first:
        before_ref = refs.pop(0)
    if last:
        weight_ref, out_ref = (refs.pop(0) for _ in range(2))
        acc_ref = refs.pop()
    else:
        acc_ref = refs.pop(0)
    if first:
        weight_ref = refs.pop(0)
        marks = refs.pop(0)
    stage = mark_source if staged else refs.pop(0)
    buffers = [(refs[0], refs[1]), (refs[2], refs[3])]
    count = stage.shape[-1]
    lag_half = cos_ref.shape[1]
    pairs = stations * stations
    width = buffers[0][0].shape[1]
    wide = 256
    held_rows = slice(slot_base * pairs, (slot_base + slot_count) * pairs)

    if not first:
        marks = mark_source
    if first:
        pair_weights(slots_ref, [mark_source, sources[1], sources[3], sources[5]], marks, weight_ref, slot_count, windows, stations, norm)
        acc_ref[:, 2 * lag_half :] = jnp.zeros((slot_count * pairs, LANES), jnp.float32)
    else:
        acc_ref[:, 2 * lag_half :] = before_ref[held_rows, 2 * lag_half :]

    for at, (which, part, lane) in enumerate([] if staged else views_at):
        view = sources[which] if part is None else sources[which].at[part]
        for window in range(windows):
            mark = marks[at, window]
            mark = jnp.concatenate([mark, mark], axis=0)
            for start in range(0, count, LANES):
                piece = view[window, :, lane + start : lane + start + LANES]
                stage[at, window, :, start : start + LANES] = piece.astype(jnp.float32) * mark

    index = [(slots_ref[slot_base + slot, 0], slots_ref[slot_base + slot, 1]) for slot in range(slot_count)]

    def cross(start, real_rows, imag_rows):
        for slot in range(slot_count):
            first_at, second_at = index[slot]
            for tile in range(width // wide):
                lanes = pl.ds(start + tile * wide, wide)
                held = pl.ds(tile * wide, wide)
                second = [
                    [
                        stage[second_at, window, pl.ds(part * stations, stations), lanes]
                        for part in range(2)
                    ]
                    for window in range(windows)
                ]
                for couple in range(0, stations, 2):
                    real_out = []
                    imag_out = []
                    for station in (couple, couple + 1):
                        real = imag = None
                        for window in range(windows):
                            xr = stage[first_at, window, pl.ds(station, 1), lanes]
                            xi = stage[first_at, window, pl.ds(stations + station, 1), lanes]
                            yr, yi = second[window]
                            r = xr * yr + xi * yi
                            i = xi * yr - xr * yi
                            real = r if real is None else real + r
                            imag = i if imag is None else imag + i
                        real_out.append(real)
                        imag_out.append(imag)
                    at = pl.ds(slot * pairs + couple * stations, 2 * stations)
                    real = jnp.concatenate(real_out, axis=0)
                    imag = jnp.concatenate(imag_out, axis=0)
                    real_rows[at, held] = real.astype(jnp.bfloat16)
                    imag_rows[at, held] = imag.astype(jnp.bfloat16)
                    total = real[:, :LANES]
                    for lane in range(LANES, wide, LANES):
                        total = total + real[:, lane : lane + LANES]
                    acc_ref[at, pl.ds(2 * lag_half, LANES)] += total

    def gather_lags(start, real_rows, imag_rows):
        at = pl.ds(low + start, width)
        for lane, rows, table in ((0, real_rows, cos_ref), (lag_half, imag_rows, sin_ref)):
            lanes = slice(lane, lane + lag_half)
            value = jnp.dot(rows[...], table[at, :], preferred_element_type=jnp.float32)
            if start > 0:
                value = value + acc_ref[:, lanes]
            elif not first:
                value = value + before_ref[held_rows, lanes]
            acc_ref[:, lanes] = value

    steps = count // width
    for step in range(steps):
        cross(step * width, *buffers[step % 2])
        if step > 0:
            gather_lags((step - 1) * width, *buffers[(step - 1) % 2])
    gather_lags((steps - 1) * width, *buffers[(steps - 1) % 2])
    if last:
        lay_out(acc_ref, weight_ref, out_ref, slot_base * pairs)


def chunk_call(slots, sources, views_at, mark_source, tables, before, weights, last, slot_base, slot_count, low, count, width, windows, stations, norm):
    lag_half = tables[0].shape[1]
    rows = slot_count * stations * stations
    first = before is None
    acc = jax.ShapeDtypeStruct((rows, 2 * lag_half + LANES), jnp.float32)
    operands = list(sources) + [mark_source] + list(tables)
    if not first:
        operands.append(before)
    if last:
        operands.append(weights)
    vmem = pl.BlockSpec(memory_space=pltpu.VMEM)
    stage_shape = (6, windows, 2 * stations, count)
    staged = last == jnp.float32
    scratch = [] if last else [pltpu.VMEM(stage_shape, jnp.float32)]
    scratch += [pltpu.VMEM((rows, width), jnp.bfloat16)] * 4
    outs = [acc]
    if first:
        outs.append(jax.ShapeDtypeStruct((rows, LANES), jnp.float32))
        outs.append(jax.ShapeDtypeStruct((6, windows, stations, LANES), jnp.float32))
    if last:
        outs = [jax.ShapeDtypeStruct((rows, 2 * lag_half), last)]
        if not staged:
            outs.append(jax.ShapeDtypeStruct(stage_shape, jnp.float32))
        scratch.append(pltpu.VMEM(acc.shape, jnp.float32))
    return pl.pallas_call(
        functools.partial(
            chunk_kernel,
            views_at=views_at,
            slot_count=slot_count,
            slot_base=slot_base,
            windows=windows,
            stations=stations,
            first=first,
            last=last,
            low=low,
            staged=staged,
            norm=norm,
        ),
        in_specs=[pl.BlockSpec(memory_space=pltpu.SMEM)] + [vmem] * len(operands),
        out_specs=[vmem] * len(outs),
        scratch_shapes=scratch,
        out_shape=outs,
        input_output_aliases={} if first or last else {len(operands): 0},
        cost_estimate=pl.CostEstimate(
            flops=4 * rows * count * lag_half, bytes_accessed=4 * count * lag_half, transcendentals=0
        ),
        compiler_params=pltpu.CompilerParams(vmem_limit_bytes=GRANT),
    )(slots, *operands)


def owner_stacks(spectra, window_mask, pair_slots):
    stations, windows, _, frequency_values = spectra.shape
    slot_count = pair_slots.shape[0]
    half = frequency_values // 2
    lag_half = LAGS // 2
    peers = lax.axis_size("sta")
    me = lax.axis_index("sta")
    core = me & 1
    chip = me >> 1
    core_pairs = [(i, i ^ 1) for i in range(peers)]
    near_pairs = [(i, i ^ 2) for i in range(peers)]
    far_pairs = [(i, (i + 4 - 8 * ((i // 2) % 2)) % peers) for i in range(peers)]
    split_pairs = dict(far_pairs)
    split_pairs.update({2: 0, peers - 3: peers - 1, 3: peers - 2, peers - 4: 1})
    split_pairs = sorted(split_pairs.items())
    unit_scale = lax.optimization_barrier(jnp.ones((), jnp.bfloat16))

    def rows_of(start, size):
        piece = lax.dynamic_slice_in_dim(spectra, start, size, 3)
        return (piece.transpose(1, 2, 0, 3) * unit_scale).reshape(windows, 2 * stations, size)

    splits = [half * cut // 16 for cut in CUTS]
    lead = splits[1]
    own_lead = rows_of(core * half, lead)
    valid = window_mask.astype(jnp.bfloat16).T[:, None, :, None]
    mark = jnp.broadcast_to(valid, (windows, 2, stations, LANES)).reshape(
        windows, 2 * stations, LANES
    )
    sent = jnp.concatenate([mark, rows_of((1 - core) * half, half)], axis=2)
    par = permute(sent, core_pairs)
    both = jnp.concatenate([mark[:, :stations], par[:, :stations, :LANES]], axis=1)
    par_lead = jnp.concatenate([both, par[:, :, LANES : LANES + lead]], axis=2)
    other_slots = permute(pair_slots, core_pairs)
    near = [permute(own_lead, near_pairs), permute(par_lead, near_pairs)]
    own = []
    for at in range(1, len(splits) - 1):
        low, high = splits[at], splits[at + 1]
        own.append(rows_of(core * half + low, high - low))
        piece = jnp.stack([own[-1], par[:, :, LANES + low : LANES + high]])
        if high == half:
            piece, base = lax.optimization_barrier((piece, core * half))
        near.append(permute(piece, near_pairs))
    far = [permute(piece, split_pairs if at >= 3 else far_pairs) for at, piece in enumerate(near)]

    fine = angle_tables(jnp.arange(FINE, dtype=jnp.int32), lag_half, frequency_values)
    coarse = angle_tables(
        base + FINE * jnp.arange(half // FINE, dtype=jnp.int32), lag_half, frequency_values
    )
    slots = jnp.concatenate([pair_slots, other_slots], axis=0)
    slot_chip = slots >> 1
    group = jnp.where(slot_chip == chip, 0, jnp.where(slot_chip == (chip ^ 1), 1, 2))
    other_core = ((slots & 1) != core).astype(jnp.int32)
    live = (slots[:, :1] >= 0).astype(jnp.int32)
    table = jnp.concatenate([group * 2 + other_core, live], axis=1)
    tables = lag_tables(fine, coarse)
    norm = math.sqrt(frequency_values)
    acc = weights = None
    units = [(0, 0, lead // 512 * 256), (0, lead // 512 * 256, lead)]
    mark_source = mark
    units += [(at, splits[at], splits[at + 1]) for at in range(1, len(splits) - 1)]
    for unit, (at, low, high) in enumerate(units):
        last = unit == len(units) - 1
        if at == 0:
            sources = [own_lead, par, near[0], near[1], far[0], far[1]]
            views_at = [(which, None, low + LANES * (which in (1, 3, 5))) for which in range(6)]
        else:
            sources = [own[at - 1], par, near[at + 1], far[at + 1]]
            views_at = [(0, None, 0), (1, None, LANES + low), (2, 0, 0), (2, 1, 0), (3, 0, 0), (3, 1, 0)]
        width = SUB // 2 if last or (high - low) % SUB else SUB

        def part(kind, slot_base, slots_here, stage=None):
            return chunk_call(
                table, sources if stage is None else [], views_at, mark_source if stage is None else stage, tables, acc, weights, kind,
                slot_base, slots_here, low, high - low, width, windows, stations, norm,
            )

        if last:
            theirs, stage = part(jnp.bfloat16, slot_count, slot_count)
            other = permute(theirs, core_pairs)
            (mine,) = part(jnp.float32, 0, slot_count, stage)
        elif unit == 0:
            acc, weights, mark_source = part(None, 0, 2 * slot_count)
        else:
            (acc,) = part(None, 0, 2 * slot_count)
    out = (mine + other.astype(jnp.float32)).astype(jnp.bfloat16)
    return out.reshape(slot_count, stations, stations, LAGS)


def solution(mesh):
    placed = (P(("day", "sta"), None, None, None), P(("day", "sta"), None), P("sta", None))
    return jax.shard_map(
        owner_stacks,
        mesh=mesh,
        in_specs=placed,
        out_specs=P(("day", "sta"), None, None, None),
        check_vma=False,
    )
```
